512 devices in a mesh: row: 32 (over x, z_hi, core), col: 16 (over y, z_lo).
Axes of the slice: x: 4, y: 4, z: 16 (z_hi: 4, z_lo: 4; z = z_hi * 4 + z_lo), core: 2. Of those that a mesh axis runs over, the one named last changes fastest.
Arguments:
- pair: bfloat16 [512, 512, 128], P('row', 'col'), may hold values from -6 to 6
- targets: int32 [512, 512], P('row', 'col'), may hold values from 0 to 63, as said below
- w_gate: bfloat16 [128, 512], replicated, may hold values from -0.5 to 0.5
- w_up: bfloat16 [128, 512], replicated, may hold values from -0.5 to 0.5
- w_out: bfloat16 [512, 128], replicated, may hold values from -0.25 to 0.25
- w_head: bfloat16 [128, 64], replicated, may hold values from -16 to 16
Outputs:
- d_pair: bfloat16 [512, 512, 128], P('row', 'col')
- grad_gate: float32 [128, 512], P('row', 'col')
- grad_up: float32 [128, 512], P('row', 'col')
- grad_out: float32 [512, 128], P('row', 'col')
- grad_head: float32 [128, 64], P('row', 'col')
The draws below stay inside these ranges and needn't reach their ends.
Inputs may be any that keep to these rules, and one draw needn't show every extreme that they name: symmetric: targets[i, j] equals targets[j, i].
All inputs are finite; a program needn't handle non-finite values.
Results may differ from the reference program's by a relative error of at most 0.015.
Values may be sent and summed in bfloat16 or wider, within the bound.
A program may use at most 64 MiB of HBM per device.

```python
import jax
import jax.numpy as jnp
from jax import lax

C = 128
F = 512
BINS = 64
L = 512


def draw_targets(key, part):
    full = jax.random.randint(key, (L, L), 0, BINS, dtype=jnp.int32)
    first = lax.broadcasted_iota(jnp.int32, (L, L), 0)
    second = lax.broadcasted_iota(jnp.int32, (L, L), 1)
    return jnp.where(first <= second, full, full.T)


def draw_w_head(key, part):
    base = jax.random.normal(jax.random.fold_in(key, 3), (C, BINS), jnp.float32) * 0.2
    return jnp.clip(base, -16.0, 16.0).astype(jnp.bfloat16)


def strengthened(values, key, source, target, parts, factor):
    def block_of(position):
        return (jnp.arange(values.shape[position]) // (values.shape[position] // parts)).reshape((-1,) + (1,) * (values.ndim - 1 - position))

    near = jax.random.permutation(key, parts)[block_of(target)]
    other_side = (block_of(target) + parts // 2) % parts
    return jnp.where((block_of(source) == near) | (block_of(source) == other_side), factor * values, values)


def level_of(stream_key, shape, shards, low, top_value):
    gain, own = 1.0, jax.random.fold_in(stream_key, 6)
    for position, blocks in shards:
        heights = jnp.exp(jax.random.uniform(jax.random.fold_in(own, position), (blocks,), jnp.float32, low / len(shards), top_value / len(shards)))
        gain = gain * jnp.repeat(heights, shape[position] // blocks).reshape([-1 if axis == position else 1 for axis in range(len(shape))])
    return gain


def normal_values(key, shape, spread, most, shards=(), kind=jnp.bfloat16):
    drawn = jax.random.normal(key, shape, jnp.float32) * spread
    if len(shards) > 0:
        drawn = level_of(key, shape, shards, -0.22, 0.18) * drawn
    return jnp.clip(drawn, min=-most, max=most).astype(kind)


def heavy_noise(own_key, extent, spread, bound, split, heavy, kind=jnp.bfloat16):
    array = spread * jax.random.normal(own_key, extent, jnp.float32)
    if split:
        array = array * level_of(own_key, extent, split, -0.22, 0.18)
    return jnp.clip(strengthened(array, jax.random.fold_in(own_key, 3), *heavy), -bound, bound).astype(kind)


def setup_inputs(seed: int = 0) -> dict:
    splits = jax.random.split(jax.random.key(seed), 7)
    return {
        "pair": heavy_noise(splits[0], (L, L, C), 1.0, 6.0, ((0, 32), (1, 16)), (0, 2, 32, 2.75)),
        "targets": draw_targets(jax.random.fold_in(splits[6], 71), 0),
        "w_gate": normal_values(splits[2], (C, F), C ** -0.5, 0.5),
        "w_up": normal_values(splits[3], (C, F), C ** -0.5, 0.5),
        "w_out": normal_values(splits[4], (F, C), F ** -0.5, 0.25),
        "w_head": draw_w_head(jax.random.fold_in(splits[6], 71), 0),
    }


eps = 1e-05

def normalize(flat):
    values = flat.astype(jnp.float32)
    centre = values - lax.optimization_barrier(jnp.mean(values, axis=-1, keepdims=True))
    scale_inv = lax.rsqrt(lax.optimization_barrier(jnp.mean(centre * centre, axis=-1, keepdims=True)) + eps)
    return (centre * scale_inv, scale_inv)

def forward_block(flat, w_gate, w_up, w_out, w_head):
    normed, scale_inv = normalize(flat)
    inputs = normed.astype(jnp.bfloat16)
    gate = jnp.dot(inputs, w_gate, preferred_element_type=jnp.float32)
    upper = jnp.dot(inputs, w_up, preferred_element_type=jnp.float32)
    hidden = (jax.nn.silu(gate) * upper).astype(jnp.bfloat16)
    updated = (flat.astype(jnp.float32) + jnp.dot(hidden, w_out, preferred_element_type=jnp.float32)).astype(jnp.bfloat16)
    logits = jnp.dot(updated, w_head, preferred_element_type=jnp.float32).astype(jnp.bfloat16)
    return (updated, logits)

def backward_block(flat, updated, cotangent, w_gate, w_up, w_out, w_head):
    normed, scale_inv = normalize(flat)
    inputs = normed.astype(jnp.bfloat16)
    gate = jnp.dot(inputs, w_gate, preferred_element_type=jnp.float32)
    upper = jnp.dot(inputs, w_up, preferred_element_type=jnp.float32)
    sigma = jax.nn.sigmoid(gate)
    swish = jax.nn.silu(gate)
    hidden = (swish * upper).astype(jnp.bfloat16)
    d_updated = jnp.dot(cotangent, w_head.T, preferred_element_type=jnp.float32)
    d_upd_b = d_updated.astype(jnp.bfloat16)
    d_hidden = jnp.dot(d_upd_b, w_out.T, preferred_element_type=jnp.float32)
    d_gate = (d_hidden * upper * sigma * (1.0 + gate * (1.0 - sigma))).astype(jnp.bfloat16)
    d_up = (d_hidden * swish).astype(jnp.bfloat16)
    d_inputs = jnp.dot(d_gate, w_gate.T, preferred_element_type=jnp.float32) + jnp.dot(d_up, w_up.T, preferred_element_type=jnp.float32)
    d_norm = (d_inputs - lax.optimization_barrier(jnp.mean(d_inputs, axis=-1, keepdims=True)) - normed * lax.optimization_barrier(jnp.mean(d_inputs * normed, axis=-1, keepdims=True))) * scale_inv
    d_block = (d_updated + d_norm).astype(jnp.bfloat16)
    terms = (jnp.dot(inputs.T, d_gate, preferred_element_type=jnp.float32), jnp.dot(inputs.T, d_up, preferred_element_type=jnp.float32), jnp.dot(hidden.T, d_upd_b, preferred_element_type=jnp.float32), jnp.dot(updated.T, cotangent, preferred_element_type=jnp.float32))
    return (terms, d_block)

def reference(pair, targets, w_gate, w_up, w_out, w_head):
    length = pair.shape[0]
    width = pair.shape[2]
    bins = w_head.shape[1]
    rows_step = 8
    nblocks = length // rows_step
    blocks = pair.reshape(nblocks, rows_step * length, width)
    updated, logits = lax.map(lambda blk: forward_block(blk, w_gate, w_up, w_out, w_head), blocks)
    logits = logits.reshape(length, length, bins)
    summed = logits.astype(jnp.float32) + jnp.transpose(logits, (1, 0, 2)).astype(jnp.float32)
    probs = jax.nn.softmax(summed, axis=-1)
    onehot = (targets[:, :, None] == jnp.arange(bins, dtype=jnp.int32)[None, None, :]).astype(jnp.float32)
    grad_sym = (probs - onehot).astype(jnp.bfloat16)
    cotangent = (grad_sym.astype(jnp.float32) + jnp.transpose(grad_sym, (1, 0, 2)).astype(jnp.float32)).astype(jnp.bfloat16)
    cotangent = cotangent.reshape(nblocks, rows_step * length, bins)

    def accumulate(carry, items):
        flat, upd, cot = items
        terms, d_block = backward_block(flat, upd, cot, w_gate, w_up, w_out, w_head)
        return (tuple((c + t for c, t in zip(carry, terms))), d_block)
    start = (jnp.zeros(w_gate.shape, jnp.float32), jnp.zeros(w_up.shape, jnp.float32), jnp.zeros(w_out.shape, jnp.float32), jnp.zeros(w_head.shape, jnp.float32))
    totals, d_blocks = lax.scan(accumulate, start, (blocks, updated, cotangent))
    d_pair = d_blocks.reshape(length, length, width)
    factor = 1.0 / length
    return (d_pair, totals[0] * factor, totals[1] * factor, totals[2] * factor, totals[3] * factor)
```

```python
import functools

import jax
import jax.numpy as jnp
from jax import lax
from jax.experimental import pallas as pl
from jax.experimental.pallas import tpu as pltpu
from jax.sharding import PartitionSpec as P

MESH = pl.DeviceIdType.MESH
F32 = jnp.float32
BF16 = jnp.bfloat16
eps = 1e-05

NX = NY = NZH = NZL = 4
XY_ORDER = sorted(
    range(1, 16), key=lambda k: -(min(k // 4, 4 - k // 4) + min(k % 4, 4 - k % 4))
)
Z_ORDER = sorted(range(1, 16), key=lambda k: -min(k, 16 - k))


def nn(a, b):
    return jnp.dot(a, b, preferred_element_type=F32)


def nt(a, b):
    return lax.dot_general(a, b, (((1,), (1,)), ((), ())), preferred_element_type=F32)


def tn(a, b):
    return lax.dot_general(a, b, (((0,), (0,)), ((), ())), preferred_element_type=F32)


def kernel(
    pair_in,
    tgt_in,
    wg_in,
    wu_in,
    wo_in,
    wh_in,
    dp_out,
    gg_out,
    gu_out,
    go_out,
    gh_out,
    pv,
    tv,
    wg,
    wu,
    wo,
    wh,
    wdup,
    inp,
    normed,
    sinv,
    hidden,
    swish,
    slope,
    upd,
    logit,
    mbuf,
    mrecv,
    onehot,
    cot,
    dupd,
    dupb,
    dgate,
    dup,
    dpv,
    part,
    crecv,
    xbuf,
    xrecv,
    red,
    zbuf,
    zrecv,
    fin,
    fint,
    in_sem,
    ms,
    mr,
    cs,
    cr,
    xs,
    xr,
    zs,
    zr,
    fs,
    fr,
    out_sem,
):
    r = lax.axis_index("row")
    c = lax.axis_index("col")
    x, zh, core = r // 8, (r // 2) % 4, r % 2
    y, zl = c // 4, c % 4
    z = zh * 4 + zl
    diag = c == r // 2
    other = (r + 1 - 2 * core, c)

    loads = [
        pltpu.make_async_copy(src, dst, in_sem.at[n])
        for n, (src, dst) in enumerate(
            ((pair_in, pv), (wg_in, wg), (wu_in, wu), (wo_in, wo), (wh_in, wh), (tgt_in, tv))
        )
    ]
    for load in loads:
        load.start()

    def xy_dev(k):
        return ((x + k // 4) % 4 * 8 + zh * 2 + core, (y + k % 4) % 4 * 4 + zl)

    def z_dev(k):
        to = (z + k) % 16
        return (x * 8 + to // 4 * 2 + core, y * 4 + to % 4)

    barrier = pltpu.get_barrier_semaphore()

    def greet(dev):
        pl.semaphore_signal(barrier, inc=1, device_id=dev, device_id_type=MESH)

    for h in range(2):
        pl.when(jnp.logical_not(jnp.logical_and(diag, core == h)))(
            functools.partial(greet, (2 * c + h, r // 2))
        )
    for k in Z_ORDER:
        greet(z_dev(k))
    for k in XY_ORDER:
        greet(xy_dev(k))
    greet(other)

    lane = lax.broadcasted_iota(jnp.int32, (256, 128), 1)
    prow = lax.broadcasted_iota(jnp.int32, (256, 128), 0)

    for load in loads:
        load.wait()
    dup_sel = (
        lax.broadcasted_iota(jnp.int32, (64, 128), 1) % 64
        == lax.broadcasted_iota(jnp.int32, (64, 128), 0)
    ).astype(BF16)
    wdup[...] = nn(wh[...], dup_sel).astype(BF16)
    for h in range(2):
        rows = pl.ds(h * 256, 256)
        v = pv[:, h * 16 : (h + 1) * 16, :].reshape(256, 128).astype(F32)
        centre = v - jnp.mean(v, axis=-1, keepdims=True)
        scale = lax.rsqrt(jnp.mean(centre * centre, axis=-1, keepdims=True) + eps)
        nrm = centre * scale
        normed[rows, :] = nrm
        sinv[rows, :] = jnp.broadcast_to(scale, (256, 128))
        inputs = nrm.astype(BF16)
        inp[rows, :] = inputs
        for n in range(2):
            cols = slice(n * 256, (n + 1) * 256)
            gate = nn(inputs, wg[:, cols])
            upper = nn(inputs, wu[:, cols])
            sigma = 0.5 * jnp.tanh(0.5 * gate) + 0.5
            sw = gate * sigma
            hidden[rows, cols] = (sw * upper).astype(BF16)
            swish[rows, cols] = sw
            slope[rows, cols] = upper * sigma * (1.0 + gate * (1.0 - sigma))
        updated = (v + nn(hidden[rows, :], wo[...])).astype(BF16)
        upd[rows, :] = updated
        lg = nn(updated, wdup[...])
        logit[rows, :] = lg.astype(BF16).astype(F32)
        mbuf[h] = jnp.where(lane[:128] < 64, lg[:128], lg[128:]).astype(BF16)

    pl.semaphore_wait(barrier, 33 - diag.astype(jnp.int32))

    def mirror_copy(h, slot):
        return pltpu.make_async_remote_copy(
            src_ref=mbuf.at[h],
            dst_ref=mrecv.at[slot],
            send_sem=ms.at[h],
            recv_sem=mr.at[slot],
            device_id=(2 * c + h, r // 2),
            device_id_type=MESH,
        )

    for h in range(2):
        here = jnp.logical_and(diag, core == h)

        @pl.when(jnp.logical_not(here))
        def _():
            mirror_copy(h, core).start()

        @pl.when(here)
        def _():
            mrecv[h] = mbuf[h]

    jj = prow % 16
    valid = (lane // 64) == (jj // 8)
    spread = (
        lax.broadcasted_iota(jnp.int32, (256, 16), 0) // 16
        == lax.broadcasted_iota(jnp.int32, (256, 16), 1)
    ).astype(BF16)
    by_row = nn(spread, tv[...].astype(F32).astype(BF16))
    at = lax.broadcasted_iota(jnp.int32, (256, 32), 0) % 16
    lane32 = lax.broadcasted_iota(jnp.int32, (256, 32), 1)
    ones = jnp.ones((32, 128), BF16)
    for h in range(2):
        picked = jnp.where(lane32 == at + h * 16, by_row, 0.0).astype(BF16)
        target = nn(picked, ones)
        onehot[h * 256 : (h + 1) * 256, :] = jnp.where(
            jnp.logical_and(valid, (lane % 64).astype(F32) == target), 1.0, 0.0
        )
    perm = (lane == (jj % 8) * 16 + prow // 16).astype(BF16)
    for d in range(16):
        part[1, d, 48:64, :] = jnp.zeros((16, 128), BF16)

    for h in range(2):
        here = jnp.logical_and(diag, core == h)

        @pl.when(jnp.logical_not(here))
        def _():
            mirror_copy(h, h).wait_recv()

        rows = pl.ds(h * 256, 256)
        total = jnp.where(valid, logit[rows, :] + nn(perm, mrecv[h]), -1e30)
        shifted = jnp.exp(total - jnp.max(total, axis=-1, keepdims=True))
        probs = shifted / jnp.sum(shifted, axis=-1, keepdims=True)
        grad = (probs - onehot[rows, :]).astype(BF16).astype(F32)
        cotangent = (grad + grad).astype(BF16)
        cot[rows, :] = cotangent
        d_updated = nt(cotangent, wdup[...])
        dupd[rows, :] = d_updated
        d_upd_b = d_updated.astype(BF16)
        dupb[rows, :] = d_upd_b

    g_head = tn(upd[...], cot[...])
    g_head = g_head + pltpu.roll(g_head, 64, 1)
    for a in range(4):
        packed = jnp.where(
            lane[:16] < 64, g_head[32 * a : 32 * a + 16], g_head[32 * a + 16 : 32 * a + 32]
        ).astype(BF16)
        for b in range(4):
            part[1, a * 4 + b, 32:48, :] = packed
    for a in range(4):
        g_out = tn(dupb[...], hidden[:, a * 128 : (a + 1) * 128]).astype(BF16)
        for b in range(4):
            part[1, a * 4 + b, 0:32, :] = g_out[32 * b : 32 * b + 32]

    core_copy = pltpu.make_async_remote_copy(
        src_ref=part.at[1 - core],
        dst_ref=crecv,
        send_sem=cs,
        recv_sem=cr,
        device_id=other,
        device_id_type=MESH,
    )
    pl.when(core == 0)(core_copy.start)

    for h in range(2):
        rows = pl.ds(h * 256, 256)
        for n in range(2):
            cols = slice(n * 256, (n + 1) * 256)
            d_hidden = nt(dupb[rows, :], wo[cols, :])
            dgate[rows, cols] = (d_hidden * slope[rows, cols]).astype(BF16)
            dup[rows, cols] = (d_hidden * swish[rows, cols]).astype(BF16)
    for b in range(4):
        cols = slice(b * 128, (b + 1) * 128)
        g_gate = tn(inp[...], dgate[:, cols]).astype(BF16)
        g_up = tn(inp[...], dup[:, cols]).astype(BF16)
        for a in range(4):
            part[0, a * 4 + b, 0:32, :] = g_gate[32 * a : 32 * a + 32]
            part[0, a * 4 + b, 32:64, :] = g_up[32 * a : 32 * a + 32]
    pl.when(core == 1)(core_copy.start)

    core_copy.wait_recv()
    for d in range(16):
        xbuf[d] = (part[core, d].astype(F32) + crecv[d].astype(F32)).astype(BF16)

    def xy_copy(k):
        dev = xy_dev(k)
        to = (x + k // 4) % 4 * 4 + (y + k % 4) % 4
        return pltpu.make_async_remote_copy(
            src_ref=xbuf.at[to],
            dst_ref=xrecv.at[k - 1],
            send_sem=xs.at[k - 1],
            recv_sem=xr.at[k - 1],
            device_id=dev,
            device_id_type=MESH,
        )

    xy_copies = {k: xy_copy(k) for k in XY_ORDER}
    for k in XY_ORDER:
        xy_copies[k].start()

    for h in range(2):
        rows = pl.ds(h * 256, 256)
        d_inputs = nt(dgate[rows, :], wg[...]) + nt(dup[rows, :], wu[...])
        nrm = normed[rows, :]
        d_norm = (
            d_inputs
            - jnp.mean(d_inputs, axis=-1, keepdims=True)
            - nrm * jnp.mean(d_inputs * nrm, axis=-1, keepdims=True)
        ) * sinv[rows, :]
        dpv[:, h * 16 : (h + 1) * 16, :] = (
            (dupd[rows, :] + d_norm).astype(BF16).reshape(16, 16, 128)
        )

    total = xbuf[x * 4 + y].astype(F32)
    for k in reversed(XY_ORDER):
        xy_copies[k].wait_recv()
        total = total + xrecv[k - 1].astype(F32)
    red[...] = total
    for to in range(16):
        first = pl.multiple_of(8 * jnp.where(core == 0, to // 4, to % 4), 8)
        second = pl.multiple_of(32 + 8 * jnp.where(core == 0, to // 4, to // 4 % 2), 8)
        zbuf[to] = jnp.concatenate(
            [red[pl.ds(first, 8), :], red[pl.ds(second, 8), :]], axis=0
        ).astype(BF16)

    def z_copy(k):
        return pltpu.make_async_remote_copy(
            src_ref=zbuf.at[(z + k) % 16],
            dst_ref=zrecv.at[k - 1],
            send_sem=zs.at[k - 1],
            recv_sem=zr.at[k - 1],
            device_id=z_dev(k),
            device_id_type=MESH,
        )

    z_copies = {k: z_copy(k) for k in Z_ORDER}
    for k in Z_ORDER:
        z_copies[k].start()
    store = pltpu.make_async_copy(dpv, dp_out, out_sem)
    store.start()
    total = zbuf[z].astype(F32)
    for k in reversed(Z_ORDER):
        z_copies[k].wait_recv()
        total = total + zrecv[k - 1].astype(F32)
    fin[core] = total * (1.0 / 512.0)

    last = pltpu.make_async_remote_copy(
        src_ref=fin.at[core],
        dst_ref=fin.at[core],
        send_sem=fs,
        recv_sem=fr,
        device_id=other,
        device_id_type=MESH,
    )
    last.start()
    mirror_sends = []
    for h in range(2):
        here = jnp.logical_and(diag, core == h)

        @pl.when(jnp.logical_not(here))
        def _():
            mirror_copy(h, core).wait_send()

    core_copy.wait_send()
    for k in XY_ORDER:
        xy_copies[k].wait_send()
    for k in Z_ORDER:
        z_copies[k].wait_send()
    store.wait()
    last.wait_recv()

    a_tile = pltpu.roll(fin[0], (128 - 32 * zl) % 128, 1)
    b_tile = fin[1]
    gg_out[...] = jnp.where(core == 0, a_tile[0:4, :32], a_tile[4:8, :32])
    gu_out[...] = jnp.where(core == 0, a_tile[8:12, :32], a_tile[12:16, :32])
    fint[...] = jnp.transpose(b_tile[0:8])
    go_out[...] = fint[pl.ds(pl.multiple_of(32 * zh + 16 * core, 16), 16), :]
    h_tile = pltpu.roll(b_tile, (128 - (64 * (zh // 2) + 16 * y + 4 * zl)) % 128, 1)
    gh_out[...] = jnp.where(core == 0, h_tile[8:12, :4], h_tile[12:16, :4])
    last.wait_send()


def body(pair, targets, w_gate, w_up, w_out, w_head):
    vm = pltpu.VMEM
    dma = pltpu.SemaphoreType.DMA
    anywhere = pl.BlockSpec(memory_space=pl.ANY)
    vmem = pl.BlockSpec(memory_space=pltpu.VMEM)
    return pl.pallas_call(
        kernel,
        out_shape=(
            jax.ShapeDtypeStruct((16, 32, 128), BF16),
            jax.ShapeDtypeStruct((4, 32), F32),
            jax.ShapeDtypeStruct((4, 32), F32),
            jax.ShapeDtypeStruct((16, 8), F32),
            jax.ShapeDtypeStruct((4, 4), F32),
        ),
        in_specs=[anywhere] * 6,
        out_specs=(anywhere, vmem, vmem, vmem, vmem),
        scratch_shapes=[
            vm((16, 32, 128), BF16),
            vm((16, 32), jnp.int32),
            vm((128, 512), BF16),
            vm((128, 512), BF16),
            vm((512, 128), BF16),
            vm((128, 64), BF16),
            vm((128, 128), BF16),
            vm((512, 128), BF16),
            vm((512, 128), F32),
            vm((512, 128), F32),
            vm((512, 512), BF16),
            vm((512, 512), F32),
            vm((512, 512), F32),
            vm((512, 128), BF16),
            vm((512, 128), F32),
            vm((2, 128, 128), BF16),
            vm((2, 128, 128), BF16),
            vm((512, 128), F32),
            vm((512, 128), BF16),
            vm((512, 128), F32),
            vm((512, 128), BF16),
            vm((512, 512), BF16),
            vm((512, 512), BF16),
            vm((16, 32, 128), BF16),
            vm((2, 16, 64, 128), BF16),
            vm((16, 64, 128), BF16),
            vm((16, 64, 128), BF16),
            vm((15, 64, 128), BF16),
            vm((64, 128), F32),
            vm((16, 16, 128), BF16),
            vm((15, 16, 128), BF16),
            vm((2, 16, 128), F32),
            vm((128, 8), F32),
            dma((6,)),
            dma((2,)),
            dma((2,)),
            dma,
            dma,
            dma((15,)),
            dma((15,)),
            dma((15,)),
            dma((15,)),
            dma,
            dma,
            dma,
        ],
        compiler_params=pltpu.CompilerParams(collective_id=0, has_side_effects=True),
    )(pair, targets, w_gate, w_up, w_out, w_head)


def solution(mesh):
    placed = (P("row", "col", None), P("row", "col"), P(), P(), P(), P())
    return jax.shard_map(
        body,
        mesh=mesh,
        in_specs=placed,
        out_specs=(
            P("row", "col", None),
            P("row", "col"),
            P("row", "col"),
            P("row", "col"),
            P("row", "col"),
        ),
        check_vma=False,
    )
```

```python
import functools

import jax
import jax.numpy as jnp
from jax import lax
from jax.experimental import pallas as pl
from jax.experimental.pallas import tpu as pltpu
from jax.sharding import PartitionSpec as P

MESH = pl.DeviceIdType.MESH
F32 = jnp.float32
BF16 = jnp.bfloat16
eps = 1e-05

NX = NY = NZH = NZL = 4
XY_ORDER = sorted(
    range(1, 16), key=lambda k: -(min(k // 4, 4 - k // 4) + min(k % 4, 4 - k % 4))
)
Z_ORDER = sorted(
    [(k, q) for k in range(16) for q in range(2) if k + q > 0], key=lambda p: -min(p[0], 16 - p[0])
)


def nn(a, b):
    return jnp.dot(a, b, preferred_element_type=F32)


def nt(a, b):
    return lax.dot_general(a, b, (((1,), (1,)), ((), ())), preferred_element_type=F32)


def tn(a, b):
    return lax.dot_general(a, b, (((0,), (0,)), ((), ())), preferred_element_type=F32)


def kernel(
    pair_in,
    tgt_in,
    wg_in,
    wu_in,
    wo_in,
    wh_in,
    dp_out,
    fin_out,
    pv,
    tv,
    wg,
    wu,
    wo,
    wdup,
    wdup_t,
    wo_t,
    inp,
    inp_t,
    normed,
    sinv,
    hidden,
    swish,
    slope,
    upd,
    upd_t,
    logit,
    mbuf,
    mrecv,
    onehot,
    cot,
    dupd,
    dupb,
    dupb_t,
    dgate,
    dup,
    part,
    crecv,
    xbuf,
    xrecv,
    red,
    zbuf,
    zrecv,
    in_sem,
    ms,
    mr,
    cs,
    cr,
    xs,
    xr,
    zs,
    zr,
):
    r = lax.axis_index("row")
    c = lax.axis_index("col")
    x, zh, core = r // 8, (r // 2) % 4, r % 2
    y, zl = c // 4, c % 4
    z = zh * 4 + zl
    diag = c == r // 2
    other = (r + 1 - 2 * core, c)

    loads = [
        pltpu.make_async_copy(src, dst, in_sem.at[n])
        for n, (src, dst) in enumerate(
            ((pair_in, pv), (wg_in, wg), (wu_in, wu), (wo_in, wo), (wh_in, wdup_t.at[0:64]), (tgt_in, tv))
        )
    ]
    for load in loads:
        load.start()

    def xy_dev(k):
        return ((x + k // 4) % 4 * 8 + zh * 2 + core, (y + k % 4) % 4 * 4 + zl)

    def z_dev(k, q):
        to = (z + k) % 16
        return (x * 8 + to // 4 * 2 + (core + q) % 2, y * 4 + to % 4)

    barrier = pltpu.get_barrier_semaphore()

    def greet(dev):
        pl.semaphore_signal(barrier, inc=1, device_id=dev, device_id_type=MESH)

    for h in range(2):
        pl.when(jnp.logical_not(jnp.logical_and(diag, core == h)))(
            functools.partial(greet, (2 * c + h, r // 2))
        )
    for k, q in Z_ORDER:
        greet(z_dev(k, q))
    for k in XY_ORDER:
        greet(xy_dev(k))

    lane = lax.broadcasted_iota(jnp.int32, (256, 128), 1)
    prow = lax.broadcasted_iota(jnp.int32, (256, 128), 0)

    for load in loads:
        load.wait()
    wdup_t[64:128, :] = wdup_t[0:64, :]
    for h in range(2):
        rows = pl.ds(h * 256, 256)
        v = pv[:, h * 16 : (h + 1) * 16, :].reshape(256, 128).astype(F32)
        centre = v - jnp.mean(v, axis=-1, keepdims=True)
        scale = lax.rsqrt(jnp.mean(centre * centre, axis=-1, keepdims=True) + eps)
        nrm = centre * scale
        normed[rows, :] = nrm
        sinv[rows, :] = jnp.broadcast_to(scale, (256, 128))
        inputs = nrm.astype(BF16)
        inp[rows, :] = inputs
        for n in range(2):
            cols = slice(n * 256, (n + 1) * 256)
            gate = nn(inputs, wg[:, cols])
            upper = nn(inputs, wu[:, cols])
            sigma = 0.5 * jnp.tanh(0.5 * gate) + 0.5
            sw = gate * sigma
            hidden[rows, cols] = (sw * upper).astype(BF16)
            swish[rows, cols] = sw
            slope[rows, cols] = upper * sigma * (1.0 + gate * (1.0 - sigma))
        updated = (v + nn(hidden[rows, :], wo[...])).astype(BF16)
        upd[rows, :] = updated
        lg = nt(updated, wdup_t[...])
        logit[rows, :] = lg.astype(BF16).astype(F32)
        mbuf[h] = jnp.where(lane[:128] < 64, lg[:128], lg[128:]).astype(BF16)

    pl.semaphore_wait(barrier, 48 - diag.astype(jnp.int32))

    def mirror_copy(h, slot):
        return pltpu.make_async_remote_copy(
            src_ref=mbuf.at[h],
            dst_ref=mrecv.at[slot],
            send_sem=ms.at[h],
            recv_sem=mr.at[slot],
            device_id=(2 * c + h, r // 2),
            device_id_type=MESH,
        )

    for h in range(2):
        here = jnp.logical_and(diag, core == h)

        @pl.when(jnp.logical_not(here))
        def _():
            mirror_copy(h, core).start()

        @pl.when(here)
        def _():
            mrecv[h] = mbuf[h]

    jj = prow % 16
    valid = (lane // 64) == (jj // 8)
    spread = (
        lax.broadcasted_iota(jnp.int32, (256, 16), 0) // 16
        == lax.broadcasted_iota(jnp.int32, (256, 16), 1)
    ).astype(BF16)
    by_row = nn(spread, tv[...].astype(F32).astype(BF16))
    at = lax.broadcasted_iota(jnp.int32, (256, 32), 0) % 16
    lane32 = lax.broadcasted_iota(jnp.int32, (256, 32), 1)
    ones = jnp.ones((32, 128), BF16)
    for h in range(2):
        picked = jnp.where(lane32 == at + h * 16, by_row, 0.0).astype(BF16)
        target = nn(picked, ones)
        onehot[h * 256 : (h + 1) * 256, :] = jnp.where(
            jnp.logical_and(valid, (lane % 64).astype(F32) == target), 1.0, 0.0
        )
    wdup[...] = jnp.transpose(wdup_t[...])
    wo_t[...] = jnp.transpose(wo[...])
    inp_t[...] = jnp.transpose(inp[...])
    upd_t[...] = jnp.transpose(upd[...])
    perm = (lane == (jj % 8) * 16 + prow // 16).astype(BF16)
    for d in range(16):
        part[1, d, 48:64, :] = jnp.zeros((16, 128), BF16)

    for h in range(2):
        here = jnp.logical_and(diag, core == h)

        @pl.when(jnp.logical_not(here))
        def _():
            mirror_copy(h, h).wait_recv()

        rows = pl.ds(h * 256, 256)
        total = jnp.where(valid, logit[rows, :] + nn(perm, mrecv[h]), -1e30)
        shifted = jnp.exp(total - jnp.max(total, axis=-1, keepdims=True))
        probs = shifted / jnp.sum(shifted, axis=-1, keepdims=True)
        grad = (probs - onehot[rows, :]).astype(BF16).astype(F32)
        cotangent = (grad + grad).astype(BF16)
        cot[rows, :] = cotangent
        d_updated = nn(cotangent, wdup_t[...])
        dupd[rows, :] = d_updated
        dupb[rows, :] = d_updated.astype(BF16)

    core_copy = pltpu.make_async_remote_copy(
        src_ref=part.at[1 - core],
        dst_ref=crecv,
        send_sem=cs,
        recv_sem=cr,
        device_id=other,
        device_id_type=MESH,
    )

    def out_and_head():
        dupb_t[...] = nt(wdup[...], cot[...]).astype(BF16)
        g_head = nn(upd_t[...], cot[...])
        g_head = g_head + pltpu.roll(g_head, 64, 1)
        for a in range(4):
            packed = jnp.where(
                lane[:16] < 64, g_head[32 * a : 32 * a + 16], g_head[32 * a + 16 : 32 * a + 32]
            ).astype(BF16)
            for b in range(4):
                part[1, a * 4 + b, 32:48, :] = packed
        for a in range(4):
            g_out = nn(dupb_t[...], hidden[:, a * 128 : (a + 1) * 128]).astype(BF16)
            for b in range(4):
                part[1, a * 4 + b, 0:32, :] = g_out[32 * b : 32 * b + 32]

    def gate_and_up():
        for h in range(2):
            rows = pl.ds(h * 256, 256)
            for n in range(2):
                cols = slice(n * 256, (n + 1) * 256)
                d_hidden = nn(dupb[rows, :], wo_t[:, cols])
                dgate[rows, cols] = (d_hidden * slope[rows, cols]).astype(BF16)
                dup[rows, cols] = (d_hidden * swish[rows, cols]).astype(BF16)
        for b in range(4):
            cols = slice(b * 128, (b + 1) * 128)
            g_gate = nn(inp_t[...], dgate[:, cols]).astype(BF16)
            g_up = nn(inp_t[...], dup[:, cols]).astype(BF16)
            for a in range(4):
                part[0, a * 4 + b, 0:32, :] = g_gate[32 * a : 32 * a + 32]
                part[0, a * 4 + b, 32:64, :] = g_up[32 * a : 32 * a + 32]

    @pl.when(core == 0)
    def _():
        out_and_head()
        core_copy.start()
        gate_and_up()

    @pl.when(core == 1)
    def _():
        gate_and_up()
        core_copy.start()
        out_and_head()

    core_copy.wait_recv()
    for d in range(16):
        xbuf[d] = (part[core, d].astype(F32) + crecv[d].astype(F32)).astype(BF16)

    def xy_copy(k):
        dev = xy_dev(k)
        to = (x + k // 4) % 4 * 4 + (y + k % 4) % 4
        return pltpu.make_async_remote_copy(
            src_ref=xbuf.at[to],
            dst_ref=xrecv.at[k - 1],
            send_sem=xs.at[k - 1],
            recv_sem=xr.at[k - 1],
            device_id=dev,
            device_id_type=MESH,
        )

    xy_copies = {k: xy_copy(k) for k in XY_ORDER}
    for k in XY_ORDER:
        xy_copies[k].start()

    for h in range(2):
        rows = pl.ds(h * 256, 256)
        d_inputs = nt(dgate[rows, :], wg[...]) + nt(dup[rows, :], wu[...])
        nrm = normed[rows, :]
        d_norm = (
            d_inputs
            - jnp.mean(d_inputs, axis=-1, keepdims=True)
            - nrm * jnp.mean(d_inputs * nrm, axis=-1, keepdims=True)
        ) * sinv[rows, :]
        dp_out[:, h * 16 : (h + 1) * 16, :] = (
            (dupd[rows, :] + d_norm).astype(BF16).reshape(16, 16, 128)
        )

    total = xbuf[x * 4 + y].astype(F32)
    for k in reversed(XY_ORDER):
        xy_copies[k].wait_recv()
        total = total + xrecv[k - 1].astype(F32)
    red[...] = total
    half = lane[:8] // 64
    for to in range(16):
        own = jnp.where(core == 0, to // 4, to % 4)
        keep = jnp.where(core == 0, to % 4 // 2, to // 4 // 2)
        first = pl.multiple_of(8 * own, 8)
        second = pl.multiple_of(32 + 8 * jnp.where(core == 0, to // 4, to // 4 % 2), 8)
        zbuf[to] = jnp.where(
            half == keep, red[pl.ds(first, 8), :], pltpu.roll(red[pl.ds(second, 8), :], 64, 1)
        ).astype(BF16)

    def z_copy(k, q):
        return pltpu.make_async_remote_copy(
            src_ref=zbuf.at[(z + k) % 16],
            dst_ref=zrecv.at[core, k],
            send_sem=zs.at[q, k],
            recv_sem=zr.at[core, k],
            device_id=z_dev(k, q),
            device_id_type=MESH,
        )

    def z_arrival(k, p):
        return pltpu.make_async_remote_copy(
            src_ref=zbuf.at[k],
            dst_ref=zrecv.at[p, k],
            send_sem=zs.at[0, k],
            recv_sem=zr.at[p, k],
            device_id=other,
            device_id_type=MESH,
        )

    z_copies = [z_copy(k, q) for k, q in Z_ORDER]
    for copy in z_copies:
        copy.start()
    zrecv[core, 0] = zbuf[z]
    z_arrival(0, 1 - core).wait_recv()
    total = zrecv[:, 0].astype(F32)
    for k in sorted(range(1, 16), key=lambda k: min(k, 16 - k)):
        z_arrival(k, 0).wait_recv()
        z_arrival(k, 1).wait_recv()
        total = total + zrecv[:, k].astype(F32)
    fin_out[...] = total * (1.0 / 512.0)

    for h in range(2):
        here = jnp.logical_and(diag, core == h)

        @pl.when(jnp.logical_not(here))
        def _():
            mirror_copy(h, core).wait_send()

    core_copy.wait_send()
    for k in XY_ORDER:
        xy_copies[k].wait_send()
    for copy in z_copies:
        copy.wait_send()


def finish(dp_in, fin, dp_out, gg_out, gu_out, go_out, gh_out, sem):
    store = pltpu.make_async_copy(dp_in, dp_out, sem)
    store.start()
    r = lax.axis_index("row")
    c = lax.axis_index("col")
    zh, core, y, zl = (r // 2) % 4, r % 2, c // 4, c % 4
    a_tile = pltpu.roll(fin[0], (128 - 32 * zl) % 128, 1)
    gg_out[...] = jnp.where(core == 0, a_tile[0:4, 0:32], a_tile[4:8, 0:32])
    gu_out[...] = jnp.where(core == 0, a_tile[0:4, 64:96], a_tile[4:8, 64:96])
    b_tile = fin[1]
    go_out[...] = pltpu.roll(b_tile, (128 - (32 * zh + 16 * core)) % 128, 1)[:, :16]
    h_tile = pltpu.roll(b_tile, (192 - (64 * (zh // 2) + 16 * y + 4 * zl)) % 128, 1)
    gh_out[...] = jnp.where(core == 0, h_tile[0:4, :4], h_tile[4:8, :4])
    store.wait()


def body(pair, targets, w_gate, w_up, w_out, w_head):
    vm = pltpu.VMEM
    dma = pltpu.SemaphoreType.DMA
    anywhere = pl.BlockSpec(memory_space=pl.ANY)
    vmem = pl.BlockSpec(memory_space=pltpu.VMEM)
    d_pair, fin = pl.pallas_call(
        kernel,
        out_shape=(
            pltpu.VMEM((16, 32, 128), BF16),
            pltpu.VMEM((2, 8, 128), F32),
        ),
        in_specs=[anywhere] * 6,
        out_specs=(vmem, vmem),
        scratch_shapes=[
            vm((16, 32, 128), BF16),
            vm((16, 32), jnp.int32),
            vm((128, 512), BF16),
            vm((128, 512), BF16),
            vm((512, 128), BF16),
            vm((128, 128), BF16),
            vm((128, 128), BF16),
            vm((128, 512), BF16),
            vm((512, 128), BF16),
            vm((128, 512), BF16),
            vm((512, 128), F32),
            vm((512, 128), F32),
            vm((512, 512), BF16),
            vm((512, 512), F32),
            vm((512, 512), F32),
            vm((512, 128), BF16),
            vm((128, 512), BF16),
            vm((512, 128), F32),
            vm((2, 128, 128), BF16),
            vm((2, 128, 128), BF16),
            vm((512, 128), F32),
            vm((512, 128), BF16),
            vm((512, 128), F32),
            vm((512, 128), BF16),
            vm((128, 512), BF16),
            vm((512, 512), BF16),
            vm((512, 512), BF16),
            vm((2, 16, 64, 128), BF16),
            vm((16, 64, 128), BF16),
            vm((16, 64, 128), BF16),
            vm((15, 64, 128), BF16),
            vm((64, 128), F32),
            vm((16, 8, 128), BF16),
            vm((2, 16, 8, 128), BF16),
            dma((6,)),
            dma((2,)),
            dma((2,)),
            dma,
            dma,
            dma((15,)),
            dma((15,)),
            dma((2, 16)),
            dma((2, 16)),
        ],
        compiler_params=pltpu.CompilerParams(
            collective_id=0, has_side_effects=True
        ),
    )(pair, targets, w_gate, w_up, w_out, w_head.T)
    d_pair, g_gate, g_up, g_out, g_head = pl.pallas_call(
        finish,
        out_shape=(
            jax.ShapeDtypeStruct((16, 32, 128), BF16),
            jax.ShapeDtypeStruct((4, 32), F32),
            jax.ShapeDtypeStruct((4, 32), F32),
            jax.ShapeDtypeStruct((8, 16), F32),
            jax.ShapeDtypeStruct((4, 4), F32),
        ),
        in_specs=[vmem, vmem],
        out_specs=(anywhere, vmem, vmem, vmem, vmem),
        scratch_shapes=[dma],
        compiler_params=pltpu.CompilerParams(vmem_limit_bytes=16 * 2**20),
    )(d_pair, fin)
    return d_pair, g_gate, g_up, g_out.T, g_head


def solution(mesh):
    placed = (P("row", "col", None), P("row", "col"), P(), P(), P(), P())
    return jax.shard_map(
        body,
        mesh=mesh,
        in_specs=placed,
        out_specs=(
            P("row", "col", None),
            P("row", "col"),
            P("row", "col"),
            P("row", "col"),
            P("row", "col"),
        ),
        check_vma=False,
    )
```

```python
import functools

import jax
import jax.numpy as jnp
from jax import lax
from jax.experimental import pallas as pl
from jax.experimental.pallas import tpu as pltpu
from jax.sharding import PartitionSpec as P

MESH = pl.DeviceIdType.MESH
F32 = jnp.float32
BF16 = jnp.bfloat16
eps = 1e-05

NX = NY = NZH = NZL = 4
XY_ORDER = sorted(
    range(1, 16), key=lambda k: -(min(k // 4, 4 - k // 4) + min(k % 4, 4 - k % 4))
)
Z_ORDER = sorted(
    [(k, q) for k in range(16) for q in range(2) if k + q > 0], key=lambda p: -min(p[0], 16 - p[0])
)
Z_LEVEL = [0, 0, 0, 0, 0, 3, 3, 3, 2, 3, 3, 3, 1, 3, 3, 3]
Z_MATES = [sum(v <= level for v in Z_LEVEL) - 1 for level in range(4)]
XY_LIST = sorted(
    range(16), key=lambda t: (min(t // 4, 4 - t // 4) + min(t % 4, 4 - t % 4), t)
)
XY_PLACE = [XY_LIST.index(t) for t in range(16)]


def look_up(table, at):
    found = 0
    for n, value in enumerate(table):
        found = jnp.where(at == n, value, found)
    return found


def nn(a, b):
    return jnp.dot(a, b, preferred_element_type=F32)


def nt(a, b):
    return lax.dot_general(a, b, (((1,), (1,)), ((), ())), preferred_element_type=F32)


def tn(a, b):
    return lax.dot_general(a, b, (((0,), (0,)), ((), ())), preferred_element_type=F32)


def kernel(
    pair_in,
    tgt_in,
    wg_in,
    wu_in,
    wo_in,
    wh_in,
    dp_out,
    fin_out,
    pv,
    tv,
    wg,
    wu,
    wo,
    wdup,
    wdup_t,
    wo_t,
    inp,
    inp_t,
    normed,
    sinv,
    hidden,
    swish,
    slope,
    upd,
    upd_t,
    logit,
    mbuf,
    mrecv,
    onehot,
    cot,
    dupd,
    dupb,
    dupb_t,
    dgate,
    dup,
    part,
    crecv,
    xbuf,
    xrecv,
    red,
    zbuf,
    zrecv,
    in_sem,
    ms,
    mr,
    cs,
    cr,
    xs,
    xr,
    zs,
    zr,
    rbuf,
    rs_send,
    rs_recv,
    fw_send,
    near,
    along,
    far,
):
    r = lax.axis_index("row")
    c = lax.axis_index("col")
    chip, core = lax.div(r, 2), lax.rem(r, 2)
    x, zh = lax.div(chip, 4), lax.rem(chip, 4)
    y, zl = lax.div(c, 4), lax.rem(c, 4)
    z, z_swap = zh * 4 + zl, zl * 4 + zh
    rank, rank_swap = look_up(Z_LEVEL, z), look_up(Z_LEVEL, z_swap)
    mates = look_up(Z_MATES, rank)
    place_xy = look_up(XY_PLACE, x * 4 + y)
    first, late, level = rank < rank_swap, rank > rank_swap, z == z_swap
    relayed = jnp.logical_and(first, x != y)
    crossed = jnp.logical_and(z != z_swap, x != y)
    direct = jnp.logical_and(z != z_swap, jnp.logical_not(first))
    diag = c == chip
    other = (r + 1 - 2 * core, c)

    loads = [
        pltpu.make_async_copy(src, dst, in_sem.at[n])
        for n, (src, dst) in enumerate(
            ((pair_in, pv), (wg_in, wg), (wu_in, wu), (wo_in, wo), (wh_in, wdup_t.at[0:64]), (tgt_in, tv))
        )
    ]
    for load in loads:
        load.start()

    def xy_dev(k):
        return ((x + k // 4) % 4 * 8 + zh * 2 + core, (y + k % 4) % 4 * 4 + zl)

    def z_dev(k, q):
        to = (z + k) % 16
        return (x * 8 + to // 4 * 2 + (core + q) % 2, y * 4 + to % 4)

    barrier = pltpu.get_barrier_semaphore()

    def tell(sem, dev):
        pl.semaphore_signal(sem, inc=1, device_id=dev, device_id_type=MESH)

    def wait_some(sem, count):
        @pl.when(count > 0)
        def _():
            pl.semaphore_wait(sem, count)

    def z_mates(t):
        row = x * 8 + t // 4 * 2
        return ((row, y * 4 + t % 4), (row + 1, y * 4 + t % 4))

    def xy_mate(t):
        return (t // 4 * 8 + zh * 2 + core, t % 4 * 4 + zl)

    turned = (y * 8 + zh * 2 + 1 - core, x * 4 + zl)

    @pl.when(jnp.logical_and(crossed, jnp.logical_not(late)))
    def _():
        for h in range(2):
            tell(barrier, (2 * c + h, chip))

    for t in range(16):

        @pl.when(jnp.logical_and(Z_LEVEL[t] >= rank, z != t))
        def _():
            for dev in z_mates(t):
                tell(barrier, dev)

    for t in range(16):

        @pl.when(XY_PLACE[t] > place_xy)
        def _():
            tell(barrier, xy_mate(t))

    @pl.when(x < y)
    def _():
        tell(barrier, turned)

    tell(barrier, other)

    lane = lax.broadcasted_iota(jnp.int32, (256, 128), 1)
    prow = lax.broadcasted_iota(jnp.int32, (256, 128), 0)

    for load in loads:
        load.wait()
    wdup_t[64:128, :] = wdup_t[0:64, :]
    for h in range(2):
        rows = pl.ds(h * 256, 256)
        v = pv[:, h * 16 : (h + 1) * 16, :].reshape(256, 128).astype(F32)
        centre = v - jnp.mean(v, axis=-1, keepdims=True)
        scale = lax.rsqrt(jnp.mean(centre * centre, axis=-1, keepdims=True) + eps)
        nrm = centre * scale
        normed[rows, :] = nrm
        sinv[rows, :] = jnp.broadcast_to(scale, (256, 128))
        inputs = nrm.astype(BF16)
        inp[rows, :] = inputs
        for n in range(2):
            cols = slice(n * 256, (n + 1) * 256)
            gate = nn(inputs, wg[:, cols])
            upper = nn(inputs, wu[:, cols])
            sigma = 0.5 * jnp.tanh(0.5 * gate) + 0.5
            sw = gate * sigma
            hidden[rows, cols] = (sw * upper).astype(BF16)
            swish[rows, cols] = sw
            slope[rows, cols] = upper * sigma * (1.0 + gate * (1.0 - sigma))
        updated = (v + nn(hidden[rows, :], wo[...])).astype(BF16)
        upd[rows, :] = updated
        lg = nt(updated, wdup_t[...])
        logit[rows, :] = lg.astype(BF16).astype(F32)
        mbuf[h] = jnp.where(lane[:128] < 64, lg[:128], lg[128:]).astype(BF16)

    pl.semaphore_wait(
        barrier,
        2 * mates
        + place_xy
        + (y < x).astype(jnp.int32)
        + 1
        + 2 * jnp.logical_and(crossed, jnp.logical_not(first)).astype(jnp.int32),
    )

    @pl.when(late)
    def _():
        for h in range(2):
            tell(far, (x * 8 + zl * 2 + h, y * 4 + zh))

    def mirror_copy(h, slot):
        return pltpu.make_async_remote_copy(
            src_ref=mbuf.at[h],
            dst_ref=mrecv.at[slot],
            send_sem=ms.at[h],
            recv_sem=mr.at[slot],
            device_id=(2 * c + h, chip),
            device_id_type=MESH,
        )

    def relay_copy(h, slot):
        return pltpu.make_async_remote_copy(
            src_ref=mbuf.at[h],
            dst_ref=rbuf.at[slot],
            send_sem=rs_send.at[h],
            recv_sem=rs_recv.at[slot],
            device_id=(y * 8 + zh * 2 + h, x * 4 + zl),
            device_id_type=MESH,
        )

    def forward_copy(slot):
        return pltpu.make_async_remote_copy(
            src_ref=rbuf.at[slot],
            dst_ref=mrecv.at[slot],
            send_sem=fw_send.at[slot],
            recv_sem=mr.at[slot],
            device_id=(x * 8 + zl * 2 + core, y * 4 + zh),
            device_id_type=MESH,
        )

    @pl.when(direct)
    def _():
        for h in range(2):
            mirror_copy(h, core).start()

    for t in range(16):

        @pl.when(XY_PLACE[t] < place_xy)
        def _():
            tell(near, xy_mate(t))

    @pl.when(y < x)
    def _():
        tell(near, turned)

    for t in range(16):

        @pl.when(Z_LEVEL[t] < rank)
        def _():
            for dev in z_mates(t):
                tell(along, dev)

    wait_some(near, 15 - place_xy + (x < y).astype(jnp.int32))

    @pl.when(relayed)
    def _():
        for h in range(2):
            relay_copy(h, core).start()

    for h in range(2):
        here = jnp.logical_and(diag, core == h)

        @pl.when(jnp.logical_and(level, jnp.logical_not(here)))
        def _():
            mirror_copy(h, core).start()

        @pl.when(here)
        def _():
            mrecv[h] = mbuf[h]

    jj = prow % 16
    valid = (lane // 64) == (jj // 8)
    spread = (
        lax.broadcasted_iota(jnp.int32, (256, 16), 0) // 16
        == lax.broadcasted_iota(jnp.int32, (256, 16), 1)
    ).astype(BF16)
    by_row = nn(spread, tv[...].astype(F32).astype(BF16))
    at = lax.broadcasted_iota(jnp.int32, (256, 32), 0) % 16
    lane32 = lax.broadcasted_iota(jnp.int32, (256, 32), 1)
    ones = jnp.ones((32, 128), BF16)
    for h in range(2):
        picked = jnp.where(lane32 == at + h * 16, by_row, 0.0).astype(BF16)
        target = nn(picked, ones)
        onehot[h * 256 : (h + 1) * 256, :] = jnp.where(
            jnp.logical_and(valid, (lane % 64).astype(F32) == target), 1.0, 0.0
        )
    wdup[...] = jnp.transpose(wdup_t[...])
    wo_t[...] = jnp.transpose(wo[...])
    inp_t[...] = jnp.transpose(inp[...])
    upd_t[...] = jnp.transpose(upd[...])
    perm = (lane == (jj % 8) * 16 + prow // 16).astype(BF16)
    for d in range(16):
        part[1, d, 48:64, :] = jnp.zeros((16, 128), BF16)

    @pl.when(relayed)
    def _():
        for slot in range(2):
            relay_copy(slot, slot).wait_recv()

    wait_some(far, 2 * first.astype(jnp.int32))

    @pl.when(relayed)
    def _():
        for slot in range(2):
            forward_copy(slot).start()

    @pl.when(jnp.logical_and(first, x == y))
    def _():
        for h in range(2):
            mirror_copy(h, core).start()

    for h in range(2):
        here = jnp.logical_and(diag, core == h)

        @pl.when(jnp.logical_not(here))
        def _():
            mirror_copy(h, h).wait_recv()

        rows = pl.ds(h * 256, 256)
        total = jnp.where(valid, logit[rows, :] + nn(perm, mrecv[h]), -1e30)
        shifted = jnp.exp(total - jnp.max(total, axis=-1, keepdims=True))
        probs = shifted / jnp.sum(shifted, axis=-1, keepdims=True)
        grad = (probs - onehot[rows, :]).astype(BF16).astype(F32)
        cotangent = (grad + grad).astype(BF16)
        cot[rows, :] = cotangent
        d_updated = nn(cotangent, wdup_t[...])
        dupd[rows, :] = d_updated
        dupb[rows, :] = d_updated.astype(BF16)

    core_copy = pltpu.make_async_remote_copy(
        src_ref=part.at[1 - core],
        dst_ref=crecv,
        send_sem=cs,
        recv_sem=cr,
        device_id=other,
        device_id_type=MESH,
    )

    def out_and_head():
        dupb_t[...] = nt(wdup[...], cot[...]).astype(BF16)
        g_head = nn(upd_t[...], cot[...])
        g_head = g_head + pltpu.roll(g_head, 64, 1)
        for a in range(4):
            packed = jnp.where(
                lane[:16] < 64, g_head[32 * a : 32 * a + 16], g_head[32 * a + 16 : 32 * a + 32]
            ).astype(BF16)
            for b in range(4):
                part[1, a * 4 + b, 32:48, :] = packed
        for a in range(4):
            g_out = nn(dupb_t[...], hidden[:, a * 128 : (a + 1) * 128]).astype(BF16)
            for b in range(4):
                part[1, a * 4 + b, 0:32, :] = g_out[32 * b : 32 * b + 32]

    def gate_and_up():
        for h in range(2):
            rows = pl.ds(h * 256, 256)
            for n in range(2):
                cols = slice(n * 256, (n + 1) * 256)
                d_hidden = nn(dupb[rows, :], wo_t[:, cols])
                dgate[rows, cols] = (d_hidden * slope[rows, cols]).astype(BF16)
                dup[rows, cols] = (d_hidden * swish[rows, cols]).astype(BF16)
        for b in range(4):
            cols = slice(b * 128, (b + 1) * 128)
            g_gate = nn(inp_t[...], dgate[:, cols]).astype(BF16)
            g_up = nn(inp_t[...], dup[:, cols]).astype(BF16)
            for a in range(4):
                part[0, a * 4 + b, 0:32, :] = g_gate[32 * a : 32 * a + 32]
                part[0, a * 4 + b, 32:64, :] = g_up[32 * a : 32 * a + 32]

    @pl.when(core == 0)
    def _():
        out_and_head()
        core_copy.start()
        gate_and_up()

    @pl.when(core == 1)
    def _():
        gate_and_up()
        core_copy.start()
        out_and_head()

    core_copy.wait_recv()
    for d in range(16):
        xbuf[d] = (part[core, d].astype(F32) + crecv[d].astype(F32)).astype(BF16)

    def xy_copy(k):
        dev = xy_dev(k)
        to = (x + k // 4) % 4 * 4 + (y + k % 4) % 4
        return pltpu.make_async_remote_copy(
            src_ref=xbuf.at[to],
            dst_ref=xrecv.at[k - 1],
            send_sem=xs.at[k - 1],
            recv_sem=xr.at[k - 1],
            device_id=dev,
            device_id_type=MESH,
        )

    xy_copies = {k: xy_copy(k) for k in XY_ORDER}
    for k in XY_ORDER:
        xy_copies[k].start()

    for h in range(2):
        rows = pl.ds(h * 256, 256)
        d_inputs = nt(dgate[rows, :], wg[...]) + nt(dup[rows, :], wu[...])
        nrm = normed[rows, :]
        d_norm = (
            d_inputs
            - jnp.mean(d_inputs, axis=-1, keepdims=True)
            - nrm * jnp.mean(d_inputs * nrm, axis=-1, keepdims=True)
        ) * sinv[rows, :]
        dp_out[:, h * 16 : (h + 1) * 16, :] = (
            (dupd[rows, :] + d_norm).astype(BF16).reshape(16, 16, 128)
        )

    total = xbuf[x * 4 + y].astype(F32)
    for k in reversed(XY_ORDER):
        xy_copies[k].wait_recv()
        total = total + xrecv[k - 1].astype(F32)
    red[...] = total
    half = lane[:8] // 64
    for to in range(16):
        own = jnp.where(core == 0, to // 4, to % 4)
        keep = jnp.where(core == 0, to % 4 // 2, to // 4 // 2)
        top = pl.multiple_of(8 * own, 8)
        second = pl.multiple_of(32 + 8 * jnp.where(core == 0, to // 4, to // 4 % 2), 8)
        zbuf[to] = jnp.where(
            half == keep, red[pl.ds(top, 8), :], pltpu.roll(red[pl.ds(second, 8), :], 64, 1)
        ).astype(BF16)

    def z_copy(k, q):
        return pltpu.make_async_remote_copy(
            src_ref=zbuf.at[(z + k) % 16],
            dst_ref=zrecv.at[core, k],
            send_sem=zs.at[q, k],
            recv_sem=zr.at[core, k],
            device_id=z_dev(k, q),
            device_id_type=MESH,
        )

    def z_arrival(k, p):
        return pltpu.make_async_remote_copy(
            src_ref=zbuf.at[k],
            dst_ref=zrecv.at[p, k],
            send_sem=zs.at[0, k],
            recv_sem=zr.at[p, k],
            device_id=other,
            device_id_type=MESH,
        )

    wait_some(along, 2 * (15 - mates))
    z_copies = [z_copy(k, q) for k, q in Z_ORDER]
    for copy in z_copies:
        copy.start()
    zrecv[core, 0] = zbuf[z]
    z_arrival(0, 1 - core).wait_recv()
    total = zrecv[:, 0].astype(F32)
    for k in sorted(range(1, 16), key=lambda k: min(k, 16 - k)):
        z_arrival(k, 0).wait_recv()
        z_arrival(k, 1).wait_recv()
        total = total + zrecv[:, k].astype(F32)
    fin_out[...] = total * (1.0 / 512.0)

    @pl.when(relayed)
    def _():
        for slot in range(2):
            relay_copy(slot, core).wait_send()
            forward_copy(slot).wait_send()

    for h in range(2):
        here = jnp.logical_and(diag, core == h)

        @pl.when(jnp.logical_not(jnp.logical_or(here, relayed)))
        def _():
            mirror_copy(h, core).wait_send()

    core_copy.wait_send()
    for k in XY_ORDER:
        xy_copies[k].wait_send()
    for copy in z_copies:
        copy.wait_send()


def finish(dp_in, fin, dp_out, gg_out, gu_out, go_out, gh_out, sem):
    store = pltpu.make_async_copy(dp_in, dp_out, sem)
    store.start()
    r = lax.axis_index("row")
    c = lax.axis_index("col")
    zh, core, y, zl = (r // 2) % 4, r % 2, c // 4, c % 4
    a_tile = pltpu.roll(fin[0], (128 - 32 * zl) % 128, 1)
    gg_out[...] = jnp.where(core == 0, a_tile[0:4, 0:32], a_tile[4:8, 0:32])
    gu_out[...] = jnp.where(core == 0, a_tile[0:4, 64:96], a_tile[4:8, 64:96])
    b_tile = fin[1]
    go_out[...] = pltpu.roll(b_tile, (128 - (32 * zh + 16 * core)) % 128, 1)[:, :16]
    h_tile = pltpu.roll(b_tile, (192 - (64 * (zh // 2) + 16 * y + 4 * zl)) % 128, 1)
    gh_out[...] = jnp.where(core == 0, h_tile[0:4, :4], h_tile[4:8, :4])
    store.wait()


def body(pair, targets, w_gate, w_up, w_out, w_head):
    vm = pltpu.VMEM
    dma = pltpu.SemaphoreType.DMA
    anywhere = pl.BlockSpec(memory_space=pl.ANY)
    vmem = pl.BlockSpec(memory_space=pltpu.VMEM)
    d_pair, fin = pl.pallas_call(
        kernel,
        out_shape=(
            pltpu.VMEM((16, 32, 128), BF16),
            pltpu.VMEM((2, 8, 128), F32),
        ),
        in_specs=[anywhere] * 6,
        out_specs=(vmem, vmem),
        scratch_shapes=[
            vm((16, 32, 128), BF16),
            vm((16, 32), jnp.int32),
            vm((128, 512), BF16),
            vm((128, 512), BF16),
            vm((512, 128), BF16),
            vm((128, 128), BF16),
            vm((128, 128), BF16),
            vm((128, 512), BF16),
            vm((512, 128), BF16),
            vm((128, 512), BF16),
            vm((512, 128), F32),
            vm((512, 128), F32),
            vm((512, 512), BF16),
            vm((512, 512), F32),
            vm((512, 512), F32),
            vm((512, 128), BF16),
            vm((128, 512), BF16),
            vm((512, 128), F32),
            vm((2, 128, 128), BF16),
            vm((2, 128, 128), BF16),
            vm((512, 128), F32),
            vm((512, 128), BF16),
            vm((512, 128), F32),
            vm((512, 128), BF16),
            vm((128, 512), BF16),
            vm((512, 512), BF16),
            vm((512, 512), BF16),
            vm((2, 16, 64, 128), BF16),
            vm((16, 64, 128), BF16),
            vm((16, 64, 128), BF16),
            vm((15, 64, 128), BF16),
            vm((64, 128), F32),
            vm((16, 8, 128), BF16),
            vm((2, 16, 8, 128), BF16),
            dma((6,)),
            dma((2,)),
            dma((2,)),
            dma,
            dma,
            dma((15,)),
            dma((15,)),
            dma((2, 16)),
            dma((2, 16)),
            vm((2, 128, 128), BF16),
            dma((2,)),
            dma((2,)),
            dma((2,)),
            pltpu.SemaphoreType.REGULAR,
            pltpu.SemaphoreType.REGULAR,
            pltpu.SemaphoreType.REGULAR,
        ],
        compiler_params=pltpu.CompilerParams(
            collective_id=0, has_side_effects=True
        ),
    )(pair, targets, w_gate, w_up, w_out, w_head.T)
    d_pair, g_gate, g_up, g_out, g_head = pl.pallas_call(
        finish,
        out_shape=(
            jax.ShapeDtypeStruct((16, 32, 128), BF16),
            jax.ShapeDtypeStruct((4, 32), F32),
            jax.ShapeDtypeStruct((4, 32), F32),
            jax.ShapeDtypeStruct((8, 16), F32),
            jax.ShapeDtypeStruct((4, 4), F32),
        ),
        in_specs=[vmem, vmem],
        out_specs=(anywhere, vmem, vmem, vmem, vmem),
        scratch_shapes=[dma],
        compiler_params=pltpu.CompilerParams(vmem_limit_bytes=16 * 2**20),
    )(d_pair, fin)
    return d_pair, g_gate, g_up, g_out.T, g_head


def solution(mesh):
    placed = (P("row", "col", None), P("row", "col"), P(), P(), P(), P())
    return jax.shard_map(
        body,
        mesh=mesh,
        in_specs=placed,
        out_specs=(
            P("row", "col", None),
            P("row", "col"),
            P("row", "col"),
            P("row", "col"),
            P("row", "col"),
        ),
        check_vma=False,
    )
```

```python
import functools

import jax
import jax.numpy as jnp
from jax import lax
from jax.experimental import pallas as pl
from jax.experimental.pallas import tpu as pltpu
from jax.sharding import PartitionSpec as P

MESH = pl.DeviceIdType.MESH
F32 = jnp.float32
BF16 = jnp.bfloat16
eps = 1e-05

NX = NY = NZH = NZL = 4
XY_ORDER = sorted(
    range(1, 16), key=lambda k: -(min(k // 4, 4 - k // 4) + min(k % 4, 4 - k % 4))
)
FAR_FIRST = (2, 1, 3, 0)
Z_ORDER = sorted(
    [(k, q) for k in range(16) for q in range(2) if k + q > 0], key=lambda p: -min(p[0], 16 - p[0])
)
Z_LEVEL = [0, 0, 0, 0, 0, 3, 3, 3, 2, 3, 3, 3, 1, 3, 3, 3]
Z_MATES = [sum(v <= level for v in Z_LEVEL) - 1 for level in range(4)]
XY_LIST = sorted(
    range(16), key=lambda t: (min(t // 4, 4 - t // 4) + min(t % 4, 4 - t % 4), t)
)
XY_PLACE = [XY_LIST.index(t) for t in range(16)]


def look_up(table, at):
    found = 0
    for n, value in enumerate(table):
        found = jnp.where(at == n, value, found)
    return found


def nn(a, b):
    return jnp.dot(a, b, preferred_element_type=F32)


def nt(a, b):
    return lax.dot_general(a, b, (((1,), (1,)), ((), ())), preferred_element_type=F32)


def tn(a, b):
    return lax.dot_general(a, b, (((0,), (0,)), ((), ())), preferred_element_type=F32)


def kernel(
    pair_in,
    tgt_in,
    wg_in,
    wu_in,
    wo_in,
    wh_in,
    dp_out,
    fin_out,
    pv,
    tv,
    wg,
    wu,
    wo,
    wdup,
    wdup_t,
    wo_t,
    inp,
    inp_t,
    normed,
    sinv,
    hidden,
    swish,
    slope,
    upd,
    upd_t,
    logit,
    mbuf,
    mrecv,
    onehot,
    cot,
    dupd,
    dupb,
    dupb_t,
    dgate,
    dup,
    part_a,
    part_b,
    crecv_a,
    crecv_b,
    xbuf_a,
    xbuf_b,
    xrecv_a,
    xrecv_b,
    heads,
    red,
    zbuf,
    zrecv,
    in_sem,
    ms,
    mr,
    cs,
    cr,
    xs,
    xr,
    zs,
    zr,
    rbuf,
    rs_send,
    rs_recv,
    fw_send,
    near,
    along,
    far,
):
    r = lax.axis_index("row")
    c = lax.axis_index("col")
    chip, core = lax.div(r, 2), lax.rem(r, 2)
    x, zh = lax.div(chip, 4), lax.rem(chip, 4)
    y, zl = lax.div(c, 4), lax.rem(c, 4)
    z, z_swap = zh * 4 + zl, zl * 4 + zh
    rank, rank_swap = look_up(Z_LEVEL, z), look_up(Z_LEVEL, z_swap)
    mates = look_up(Z_MATES, rank)
    place_xy = look_up(XY_PLACE, x * 4 + y)
    first, late, level = rank < rank_swap, rank > rank_swap, z == z_swap
    relayed = jnp.logical_and(first, x != y)
    crossed = jnp.logical_and(z != z_swap, x != y)
    direct = jnp.logical_and(z != z_swap, jnp.logical_not(first))
    diag = c == chip
    other = (r + 1 - 2 * core, c)

    loads = [
        pltpu.make_async_copy(src, dst, in_sem.at[n])
        for n, (src, dst) in enumerate(
            ((pair_in, pv), (wg_in, wg), (wu_in, wu), (wo_in, wo), (wh_in, wdup_t.at[0:64]), (tgt_in, tv))
        )
    ]
    for load in loads:
        load.start()

    def xy_dev(k):
        return ((x + k // 4) % 4 * 8 + zh * 2 + core, (y + k % 4) % 4 * 4 + zl)

    def z_dev(k, q):
        to = (z + k) % 16
        return (x * 8 + to // 4 * 2 + (core + q) % 2, y * 4 + to % 4)

    barrier = pltpu.get_barrier_semaphore()

    def tell(sem, dev):
        pl.semaphore_signal(sem, inc=1, device_id=dev, device_id_type=MESH)

    def wait_some(sem, count):
        @pl.when(count > 0)
        def _():
            pl.semaphore_wait(sem, count)

    def z_mates(t):
        row = x * 8 + t // 4 * 2
        return ((row, y * 4 + t % 4), (row + 1, y * 4 + t % 4))

    def xy_mate(t):
        return (t // 4 * 8 + zh * 2 + core, t % 4 * 4 + zl)

    turned = (y * 8 + zh * 2 + 1 - core, x * 4 + zl)

    @pl.when(jnp.logical_and(crossed, jnp.logical_not(late)))
    def _():
        for h in range(2):
            tell(barrier, (2 * c + h, chip))

    for t in range(16):

        @pl.when(jnp.logical_and(Z_LEVEL[t] >= rank, z != t))
        def _():
            for dev in z_mates(t):
                tell(barrier, dev)

    for t in range(16):

        @pl.when(XY_PLACE[t] > place_xy)
        def _():
            tell(barrier, xy_mate(t))

    @pl.when(x < y)
    def _():
        tell(barrier, turned)

    tell(barrier, other)

    lane = lax.broadcasted_iota(jnp.int32, (256, 128), 1)
    prow = lax.broadcasted_iota(jnp.int32, (256, 128), 0)

    for load in loads:
        load.wait()
    wdup_t[64:128, :] = wdup_t[0:64, :]
    for h in range(2):
        rows = pl.ds(h * 256, 256)
        v = pv[:, h * 16 : (h + 1) * 16, :].reshape(256, 128).astype(F32)
        centre = v - jnp.mean(v, axis=-1, keepdims=True)
        scale = lax.rsqrt(jnp.mean(centre * centre, axis=-1, keepdims=True) + eps)
        nrm = centre * scale
        normed[rows, :] = nrm
        sinv[rows, :] = jnp.broadcast_to(scale, (256, 128))
        inputs = nrm.astype(BF16)
        inp[rows, :] = inputs
        for n in range(2):
            cols = slice(n * 256, (n + 1) * 256)
            gate = nn(inputs, wg[:, cols])
            upper = nn(inputs, wu[:, cols])
            sigma = 0.5 * jnp.tanh(0.5 * gate) + 0.5
            sw = gate * sigma
            hidden[rows, cols] = (sw * upper).astype(BF16)
            swish[rows, cols] = sw
            slope[rows, cols] = upper * sigma * (1.0 + gate * (1.0 - sigma))
        updated = (v + nn(hidden[rows, :], wo[...])).astype(BF16)
        upd[rows, :] = updated
        lg = nt(updated, wdup_t[...])
        logit[rows, :] = lg.astype(BF16).astype(F32)
        mbuf[h] = jnp.where(lane[:128] < 64, lg[:128], lg[128:]).astype(BF16)

    pl.semaphore_wait(
        barrier,
        2 * mates
        + place_xy
        + (y < x).astype(jnp.int32)
        + 1
        + 2 * jnp.logical_and(crossed, jnp.logical_not(first)).astype(jnp.int32),
    )

    @pl.when(late)
    def _():
        for h in range(2):
            tell(far, (x * 8 + zl * 2 + h, y * 4 + zh))

    def mirror_copy(h, slot):
        return pltpu.make_async_remote_copy(
            src_ref=mbuf.at[h],
            dst_ref=mrecv.at[slot],
            send_sem=ms.at[h],
            recv_sem=mr.at[slot],
            device_id=(2 * c + h, chip),
            device_id_type=MESH,
        )

    def relay_copy(h, slot):
        return pltpu.make_async_remote_copy(
            src_ref=mbuf.at[h],
            dst_ref=rbuf.at[slot],
            send_sem=rs_send.at[h],
            recv_sem=rs_recv.at[slot],
            device_id=(y * 8 + zh * 2 + h, x * 4 + zl),
            device_id_type=MESH,
        )

    def forward_copy(slot):
        return pltpu.make_async_remote_copy(
            src_ref=rbuf.at[slot],
            dst_ref=mrecv.at[slot],
            send_sem=fw_send.at[slot],
            recv_sem=mr.at[slot],
            device_id=(x * 8 + zl * 2 + core, y * 4 + zh),
            device_id_type=MESH,
        )

    @pl.when(direct)
    def _():
        for h in range(2):
            mirror_copy(h, core).start()

    for t in range(16):

        @pl.when(XY_PLACE[t] < place_xy)
        def _():
            tell(near, xy_mate(t))

    @pl.when(y < x)
    def _():
        tell(near, turned)

    for t in range(16):

        @pl.when(Z_LEVEL[t] < rank)
        def _():
            for dev in z_mates(t):
                tell(along, dev)

    wait_some(near, 15 - place_xy + (x < y).astype(jnp.int32))

    @pl.when(relayed)
    def _():
        for h in range(2):
            relay_copy(h, core).start()

    for h in range(2):
        here = jnp.logical_and(diag, core == h)

        @pl.when(jnp.logical_and(level, jnp.logical_not(here)))
        def _():
            mirror_copy(h, core).start()

        @pl.when(here)
        def _():
            mrecv[h] = mbuf[h]

    jj = prow % 16
    valid = (lane // 64) == (jj // 8)
    spread = (
        lax.broadcasted_iota(jnp.int32, (256, 16), 0) // 16
        == lax.broadcasted_iota(jnp.int32, (256, 16), 1)
    ).astype(BF16)
    by_row = nn(spread, tv[...].astype(F32).astype(BF16))
    at = lax.broadcasted_iota(jnp.int32, (256, 32), 0) % 16
    lane32 = lax.broadcasted_iota(jnp.int32, (256, 32), 1)
    ones = jnp.ones((32, 128), BF16)
    for h in range(2):
        picked = jnp.where(lane32 == at + h * 16, by_row, 0.0).astype(BF16)
        target = nn(picked, ones)
        onehot[h * 256 : (h + 1) * 256, :] = jnp.where(
            jnp.logical_and(valid, (lane % 64).astype(F32) == target), 1.0, 0.0
        )
    wdup[...] = jnp.transpose(wdup_t[...])
    wo_t[...] = jnp.transpose(wo[...])
    inp_t[...] = jnp.transpose(inp[...])
    upd_t[...] = jnp.transpose(upd[...])
    perm = (lane == (jj % 8) * 16 + prow // 16).astype(BF16)

    @pl.when(relayed)
    def _():
        for slot in range(2):
            relay_copy(slot, slot).wait_recv()

    wait_some(far, 2 * first.astype(jnp.int32))

    @pl.when(relayed)
    def _():
        for slot in range(2):
            forward_copy(slot).start()

    @pl.when(jnp.logical_and(first, x == y))
    def _():
        for h in range(2):
            mirror_copy(h, core).start()

    for h in range(2):
        here = jnp.logical_and(diag, core == h)

        @pl.when(jnp.logical_not(here))
        def _():
            mirror_copy(h, h).wait_recv()

        rows = pl.ds(h * 256, 256)
        total = jnp.where(valid, logit[rows, :] + nn(perm, mrecv[h]), -1e30)
        shifted = jnp.exp(total - jnp.max(total, axis=-1, keepdims=True))
        probs = shifted / jnp.sum(shifted, axis=-1, keepdims=True)
        grad = (probs - onehot[rows, :]).astype(BF16).astype(F32)
        cotangent = (grad + grad).astype(BF16)
        cot[rows, :] = cotangent
        d_updated = nn(cotangent, wdup_t[...])
        dupd[rows, :] = d_updated
        dupb[rows, :] = d_updated.astype(BF16)

    def core_copy(k, src, dst):
        return pltpu.make_async_remote_copy(
            src_ref=src.at[k],
            dst_ref=dst.at[k],
            send_sem=cs.at[k],
            recv_sem=cr.at[k],
            device_id=other,
            device_id_type=MESH,
        )

    def out_and_head(send):
        dupb_t[...] = nt(wdup[...], cot[...]).astype(BF16)
        g_head = nn(upd_t[...], cot[...])
        heads[...] = g_head + pltpu.roll(g_head, 64, 1)
        for k in FAR_FIRST:
            to = lax.rem(x + k, 4)
            top = pl.multiple_of(to * 32, 32)
            packed = jnp.where(
                lane[:16] < 64, heads[pl.ds(top, 16), :], heads[pl.ds(top + 16, 16), :]
            ).astype(BF16)
            cols = pl.ds(pl.multiple_of(to * 128, 128), 128)
            g_out = nn(dupb_t[...], hidden[:, cols]).astype(BF16)
            for b in range(4):
                part_b[k, b, 0:32, :] = g_out[32 * b : 32 * b + 32]
                part_b[k, b, 32:48, :] = packed
            if send:
                core_copy(k, part_b, crecv_b).start()

    def gate_and_up(send):
        for h in range(2):
            rows = pl.ds(h * 256, 256)
            for n in range(2):
                cols = slice(n * 256, (n + 1) * 256)
                d_hidden = nn(dupb[rows, :], wo_t[:, cols])
                dgate[rows, cols] = (d_hidden * slope[rows, cols]).astype(BF16)
                dup[rows, cols] = (d_hidden * swish[rows, cols]).astype(BF16)
        for k in FAR_FIRST:
            cols = pl.ds(pl.multiple_of(lax.rem(y + k, 4) * 128, 128), 128)
            g_gate = nn(inp_t[...], dgate[:, cols]).astype(BF16)
            g_up = nn(inp_t[...], dup[:, cols]).astype(BF16)
            for a in range(4):
                part_a[k, a, 0:32, :] = g_gate[32 * a : 32 * a + 32]
                part_a[k, a, 32:64, :] = g_up[32 * a : 32 * a + 32]
            if send:
                core_copy(k, part_a, crecv_a).start()

    def xy_copy(k, src, dst):
        dx, dy = k // 4, k % 4
        if src is xbuf_a:
            piece = src.at[dy, lax.rem(x + dx, 4)]
        else:
            piece = src.at[dx, lax.rem(y + dy, 4)]
        return pltpu.make_async_remote_copy(
            src_ref=piece,
            dst_ref=dst.at[k - 1],
            send_sem=xs.at[k - 1],
            recv_sem=xr.at[k - 1],
            device_id=xy_dev(k),
            device_id_type=MESH,
        )

    def spread_plane(part, crecv, xbuf, xrecv):
        for k in FAR_FIRST:
            core_copy(k, part, crecv).wait_recv()
            for n in range(4):
                xbuf[k, n] = (part[k, n].astype(F32) + crecv[k, n].astype(F32)).astype(BF16)
            for n in FAR_FIRST:
                step = n * 4 + k if xbuf is xbuf_a else k * 4 + n
                if step > 0:
                    xy_copy(step, xbuf, xrecv).start()

    def gather_plane(own, xbuf, xrecv):
        total = own.astype(F32)
        for k in reversed(XY_ORDER):
            xy_copy(k, xbuf, xrecv).wait_recv()
            total = total + xrecv[k - 1].astype(F32)
        return total

    @pl.when(core == 0)
    def _():
        out_and_head(True)
        gate_and_up(False)
        spread_plane(part_a, crecv_a, xbuf_a, xrecv_a)

    @pl.when(core == 1)
    def _():
        gate_and_up(True)
        out_and_head(False)
        spread_plane(part_b, crecv_b, xbuf_b, xrecv_b)

    for h in range(2):
        rows = pl.ds(h * 256, 256)
        d_inputs = nt(dgate[rows, :], wg[...]) + nt(dup[rows, :], wu[...])
        nrm = normed[rows, :]
        d_norm = (
            d_inputs
            - jnp.mean(d_inputs, axis=-1, keepdims=True)
            - nrm * jnp.mean(d_inputs * nrm, axis=-1, keepdims=True)
        ) * sinv[rows, :]
        dp_out[:, h * 16 : (h + 1) * 16, :] = (
            (dupd[rows, :] + d_norm).astype(BF16).reshape(16, 16, 128)
        )

    @pl.when(core == 0)
    def _():
        red[...] = gather_plane(xbuf_a[0, x], xbuf_a, xrecv_a)

    @pl.when(core == 1)
    def _():
        red[0:48, :] = gather_plane(xbuf_b[0, y], xbuf_b, xrecv_b)

    half = lane[:8] // 64
    for to in range(16):
        own = jnp.where(core == 0, to // 4, to % 4)
        keep = jnp.where(core == 0, to % 4 // 2, to // 4 // 2)
        top = pl.multiple_of(8 * own, 8)
        second = pl.multiple_of(32 + 8 * jnp.where(core == 0, to // 4, to // 4 % 2), 8)
        zbuf[to] = jnp.where(
            half == keep, red[pl.ds(top, 8), :], pltpu.roll(red[pl.ds(second, 8), :], 64, 1)
        ).astype(BF16)

    def z_copy(k, q):
        return pltpu.make_async_remote_copy(
            src_ref=zbuf.at[(z + k) % 16],
            dst_ref=zrecv.at[core, k],
            send_sem=zs.at[q, k],
            recv_sem=zr.at[core, k],
            device_id=z_dev(k, q),
            device_id_type=MESH,
        )

    def z_arrival(k, p):
        return pltpu.make_async_remote_copy(
            src_ref=zbuf.at[k],
            dst_ref=zrecv.at[p, k],
            send_sem=zs.at[0, k],
            recv_sem=zr.at[p, k],
            device_id=other,
            device_id_type=MESH,
        )

    wait_some(along, 2 * (15 - mates))
    z_copies = [z_copy(k, q) for k, q in Z_ORDER]
    for copy in z_copies:
        copy.start()
    zrecv[core, 0] = zbuf[z]
    z_arrival(0, 1 - core).wait_recv()
    total = zrecv[:, 0].astype(F32)
    for k in sorted(range(1, 16), key=lambda k: min(k, 16 - k)):
        z_arrival(k, 0).wait_recv()
        z_arrival(k, 1).wait_recv()
        total = total + zrecv[:, k].astype(F32)
    fin_out[...] = total * (1.0 / 512.0)

    @pl.when(relayed)
    def _():
        for slot in range(2):
            relay_copy(slot, core).wait_send()
            forward_copy(slot).wait_send()

    for h in range(2):
        here = jnp.logical_and(diag, core == h)

        @pl.when(jnp.logical_not(jnp.logical_or(here, relayed)))
        def _():
            mirror_copy(h, core).wait_send()

    @pl.when(core == 0)
    def _():
        for k in range(4):
            core_copy(k, part_b, crecv_b).wait_send()
        for k in XY_ORDER:
            xy_copy(k, xbuf_a, xrecv_a).wait_send()

    @pl.when(core == 1)
    def _():
        for k in range(4):
            core_copy(k, part_a, crecv_a).wait_send()
        for k in XY_ORDER:
            xy_copy(k, xbuf_b, xrecv_b).wait_send()

    for copy in z_copies:
        copy.wait_send()


def finish(
    dp_in, fin, dp_out, gg_out, gu_out, go_out, gh_out, gg, gu, go, gh, sem
):
    stores = [
        pltpu.make_async_copy(src, dst, sem.at[n])
        for n, (src, dst) in enumerate(
            ((dp_in, dp_out), (gg, gg_out), (gu, gu_out), (go, go_out), (gh, gh_out))
        )
    ]
    stores[0].start()
    r = lax.axis_index("row")
    c = lax.axis_index("col")
    chip, core = lax.div(r, 2), lax.rem(r, 2)
    zh, y, zl = lax.rem(chip, 4), lax.div(c, 4), lax.rem(c, 4)
    a_tile = pltpu.roll(fin[0], lax.rem(128 - 32 * zl, 128), 1)
    gg[...] = jnp.where(core == 0, a_tile[0:4, 0:32], a_tile[4:8, 0:32])
    gu[...] = jnp.where(core == 0, a_tile[0:4, 64:96], a_tile[4:8, 64:96])
    b_tile = fin[1]
    go[...] = pltpu.roll(b_tile, lax.rem(128 - (32 * zh + 16 * core), 128), 1)[:, :16]
    at = 64 * lax.div(zh, 2) + 16 * y + 4 * zl
    h_tile = pltpu.roll(b_tile, lax.rem(192 - at, 128), 1)
    gh[...] = jnp.where(core == 0, h_tile[0:4, :4], h_tile[4:8, :4])
    for store in stores[1:]:
        store.start()
    for store in stores:
        store.wait()


def body(pair, targets, w_gate, w_up, w_out, w_head):
    vm = pltpu.VMEM
    dma = pltpu.SemaphoreType.DMA
    anywhere = pl.BlockSpec(memory_space=pl.ANY)
    vmem = pl.BlockSpec(memory_space=pltpu.VMEM)
    d_pair, fin = pl.pallas_call(
        kernel,
        out_shape=(
            pltpu.VMEM((16, 32, 128), BF16),
            pltpu.VMEM((2, 8, 128), F32),
        ),
        in_specs=[anywhere] * 6,
        out_specs=(vmem, vmem),
        scratch_shapes=[
            vm((16, 32, 128), BF16),
            vm((16, 32), jnp.int32),
            vm((128, 512), BF16),
            vm((128, 512), BF16),
            vm((512, 128), BF16),
            vm((128, 128), BF16),
            vm((128, 128), BF16),
            vm((128, 512), BF16),
            vm((512, 128), BF16),
            vm((128, 512), BF16),
            vm((512, 128), F32),
            vm((512, 128), F32),
            vm((512, 512), BF16),
            vm((512, 512), F32),
            vm((512, 512), F32),
            vm((512, 128), BF16),
            vm((128, 512), BF16),
            vm((512, 128), F32),
            vm((2, 128, 128), BF16),
            vm((2, 128, 128), BF16),
            vm((512, 128), F32),
            vm((512, 128), BF16),
            vm((512, 128), F32),
            vm((512, 128), BF16),
            vm((128, 512), BF16),
            vm((512, 512), BF16),
            vm((512, 512), BF16),
            vm((4, 4, 64, 128), BF16),
            vm((4, 4, 48, 128), BF16),
            vm((4, 4, 64, 128), BF16),
            vm((4, 4, 48, 128), BF16),
            vm((4, 4, 64, 128), BF16),
            vm((4, 4, 48, 128), BF16),
            vm((15, 64, 128), BF16),
            vm((15, 48, 128), BF16),
            vm((128, 128), F32),
            vm((64, 128), F32),
            vm((16, 8, 128), BF16),
            vm((2, 16, 8, 128), BF16),
            dma((6,)),
            dma((2,)),
            dma((2,)),
            dma((4,)),
            dma((4,)),
            dma((15,)),
            dma((15,)),
            dma((2, 16)),
            dma((2, 16)),
            vm((2, 128, 128), BF16),
            dma((2,)),
            dma((2,)),
            dma((2,)),
            pltpu.SemaphoreType.REGULAR,
            pltpu.SemaphoreType.REGULAR,
            pltpu.SemaphoreType.REGULAR,
        ],
        compiler_params=pltpu.CompilerParams(
            collective_id=0, has_side_effects=True
        ),
    )(pair, targets, w_gate, w_up, w_out, w_head.T)
    d_pair, g_gate, g_up, g_out, g_head = pl.pallas_call(
        finish,
        out_shape=(
            jax.ShapeDtypeStruct((16, 32, 128), BF16),
            jax.ShapeDtypeStruct((4, 32), F32),
            jax.ShapeDtypeStruct((4, 32), F32),
            jax.ShapeDtypeStruct((8, 16), F32),
            jax.ShapeDtypeStruct((4, 4), F32),
        ),
        in_specs=[vmem, vmem],
        out_specs=(anywhere,) * 5,
        scratch_shapes=[vm((4, 32), F32), vm((4, 32), F32), vm((8, 16), F32), vm((4, 4), F32), dma((5,))],
        compiler_params=pltpu.CompilerParams(vmem_limit_bytes=16 * 2**20),
    )(d_pair, fin)
    return d_pair, g_gate, g_up, g_out.T, g_head


def solution(mesh):
    placed = (P("row", "col", None), P("row", "col"), P(), P(), P(), P())
    return jax.shard_map(
        body,
        mesh=mesh,
        in_specs=placed,
        out_specs=(
            P("row", "col", None),
            P("row", "col"),
            P("row", "col"),
            P("row", "col"),
            P("row", "col"),
        ),
        check_vma=False,
    )
```

```python
import functools

import jax
import jax.numpy as jnp
from jax import lax
from jax.experimental import pallas as pl
from jax.experimental.pallas import tpu as pltpu
from jax.sharding import PartitionSpec as P

MESH = pl.DeviceIdType.MESH
F32 = jnp.float32
BF16 = jnp.bfloat16
eps = 1e-05

NX = NY = NZH = NZL = 4
XY_ORDER = sorted(
    range(1, 16), key=lambda k: -(min(k // 4, 4 - k // 4) + min(k % 4, 4 - k % 4))
)
FAR_FIRST = (2, 1, 3, 0)
Z_ORDER = sorted(
    [(k, q) for k in range(16) for q in range(2) if k + q > 0], key=lambda p: -min(p[0], 16 - p[0])
)
Z_LEVEL = [0, 0, 0, 0, 0, 3, 3, 3, 2, 3, 3, 3, 1, 3, 3, 3]
Z_MATES = [sum(v <= level for v in Z_LEVEL) - 1 for level in range(4)]
XY_LIST = sorted(
    range(16), key=lambda t: (min(t // 4, 4 - t // 4) + min(t % 4, 4 - t % 4), t)
)
XY_PLACE = [XY_LIST.index(t) for t in range(16)]


def look_up(table, at):
    found = 0
    for n, value in enumerate(table):
        found = jnp.where(at == n, value, found)
    return found


def nn(a, b):
    return jnp.dot(a, b, preferred_element_type=F32)


def nt(a, b):
    return lax.dot_general(a, b, (((1,), (1,)), ((), ())), preferred_element_type=F32)


def tn(a, b):
    return lax.dot_general(a, b, (((0,), (0,)), ((), ())), preferred_element_type=F32)


def kernel(
    pair_in,
    tgt_in,
    wg_in,
    wu_in,
    wo_in,
    wh_in,
    dp_out,
    fin_out,
    pv,
    tv,
    wg,
    wu,
    wo,
    wdup,
    wdup_t,
    wo_t,
    inp,
    inp_t,
    normed,
    sinv,
    hidden,
    swish,
    slope,
    upd,
    upd_t,
    logit,
    mbuf,
    mrecv,
    onehot,
    cot,
    dupd,
    dupb,
    dupb_t,
    dgate,
    dup,
    part_a,
    part_b,
    crecv_a,
    crecv_b,
    xbuf_a,
    xbuf_b,
    xrecv_a,
    xrecv_b,
    heads,
    red,
    zbuf,
    zrecv,
    in_sem,
    ms,
    mr,
    cs,
    cr,
    xs,
    xr,
    zs,
    zr,
    rbuf,
    rs_send,
    rs_recv,
    fw_send,
    near,
    along,
    far,
):
    r = lax.axis_index("row")
    c = lax.axis_index("col")
    chip, core = lax.div(r, 2), lax.rem(r, 2)
    x, zh = lax.div(chip, 4), lax.rem(chip, 4)
    y, zl = lax.div(c, 4), lax.rem(c, 4)
    z, z_swap = zh * 4 + zl, zl * 4 + zh
    rank, rank_swap = look_up(Z_LEVEL, z), look_up(Z_LEVEL, z_swap)
    mates = look_up(Z_MATES, rank)
    place_xy = look_up(XY_PLACE, x * 4 + y)
    first, late, level = rank < rank_swap, rank > rank_swap, z == z_swap
    relayed = jnp.logical_and(first, x != y)
    crossed = jnp.logical_and(z != z_swap, x != y)
    direct = jnp.logical_and(z != z_swap, jnp.logical_not(first))
    diag = c == chip
    other = (r + 1 - 2 * core, c)

    loads = [
        pltpu.make_async_copy(src, dst, in_sem.at[n])
        for n, (src, dst) in enumerate(
            ((pair_in, pv), (wg_in, wg), (wu_in, wu), (wo_in, wo), (wh_in, wdup_t.at[0:64]), (tgt_in, tv))
        )
    ]
    for load in loads:
        load.start()

    def xy_dev(k):
        return ((x + k // 4) % 4 * 8 + zh * 2 + core, (y + k % 4) % 4 * 4 + zl)

    def z_dev(k, q):
        to = (z + k) % 16
        return (x * 8 + to // 4 * 2 + (core + q) % 2, y * 4 + to % 4)

    barrier = pltpu.get_barrier_semaphore()

    def tell(sem, dev):
        pl.semaphore_signal(sem, inc=1, device_id=dev, device_id_type=MESH)

    def wait_some(sem, count):
        @pl.when(count > 0)
        def _():
            pl.semaphore_wait(sem, count)

    def z_mates(t):
        row = x * 8 + t // 4 * 2
        return ((row, y * 4 + t % 4), (row + 1, y * 4 + t % 4))

    def xy_mate(t):
        return (t // 4 * 8 + zh * 2 + core, t % 4 * 4 + zl)

    turned = (y * 8 + zh * 2 + 1 - core, x * 4 + zl)

    @pl.when(jnp.logical_and(crossed, jnp.logical_not(late)))
    def _():
        for h in range(2):
            tell(barrier, (2 * c + h, chip))

    for t in range(16):

        @pl.when(jnp.logical_and(Z_LEVEL[t] >= rank, z != t))
        def _():
            for dev in z_mates(t):
                tell(barrier, dev)

    for t in range(16):

        @pl.when(XY_PLACE[t] > place_xy)
        def _():
            tell(barrier, xy_mate(t))

    @pl.when(x < y)
    def _():
        tell(barrier, turned)

    tell(barrier, other)

    lane = lax.broadcasted_iota(jnp.int32, (256, 128), 1)
    prow = lax.broadcasted_iota(jnp.int32, (256, 128), 0)

    for load in loads:
        load.wait()
    wdup_t[64:128, :] = wdup_t[0:64, :]
    for h in range(2):
        rows = pl.ds(h * 256, 256)
        v = pv[:, h * 16 : (h + 1) * 16, :].reshape(256, 128).astype(F32)
        centre = v - jnp.mean(v, axis=-1, keepdims=True)
        scale = lax.rsqrt(jnp.mean(centre * centre, axis=-1, keepdims=True) + eps)
        nrm = centre * scale
        normed[rows, :] = nrm
        sinv[rows, :] = jnp.broadcast_to(scale, (256, 128))
        inputs = nrm.astype(BF16)
        inp[rows, :] = inputs
        for n in range(2):
            cols = slice(n * 256, (n + 1) * 256)
            gate = nn(inputs, wg[:, cols])
            upper = nn(inputs, wu[:, cols])
            sigma = 0.5 * jnp.tanh(0.5 * gate) + 0.5
            sw = gate * sigma
            hidden[rows, cols] = (sw * upper).astype(BF16)
            swish[rows, cols] = sw
            slope[rows, cols] = upper * sigma * (1.0 + gate * (1.0 - sigma))
        updated = (v + nn(hidden[rows, :], wo[...])).astype(BF16)
        upd[rows, :] = updated
        lg = nt(updated, wdup_t[...])
        logit[rows, :] = lg.astype(BF16).astype(F32)
        mbuf[h] = jnp.where(lane[:128] < 64, lg[:128], lg[128:]).astype(BF16)

    pl.semaphore_wait(
        barrier,
        2 * mates
        + place_xy
        + (y < x).astype(jnp.int32)
        + 1
        + 2 * jnp.logical_and(crossed, jnp.logical_not(first)).astype(jnp.int32),
    )

    @pl.when(late)
    def _():
        for h in range(2):
            tell(far, (x * 8 + zl * 2 + h, y * 4 + zh))

    def mirror_copy(h, slot):
        return pltpu.make_async_remote_copy(
            src_ref=mbuf.at[h],
            dst_ref=mrecv.at[slot],
            send_sem=ms.at[h],
            recv_sem=mr.at[slot],
            device_id=(2 * c + h, chip),
            device_id_type=MESH,
        )

    def relay_copy(h, slot):
        return pltpu.make_async_remote_copy(
            src_ref=mbuf.at[h],
            dst_ref=rbuf.at[slot],
            send_sem=rs_send.at[h],
            recv_sem=rs_recv.at[slot],
            device_id=(y * 8 + zh * 2 + h, x * 4 + zl),
            device_id_type=MESH,
        )

    def forward_copy(slot):
        return pltpu.make_async_remote_copy(
            src_ref=rbuf.at[slot],
            dst_ref=mrecv.at[slot],
            send_sem=fw_send.at[slot],
            recv_sem=mr.at[slot],
            device_id=(x * 8 + zl * 2 + core, y * 4 + zh),
            device_id_type=MESH,
        )

    @pl.when(direct)
    def _():
        for h in range(2):
            mirror_copy(h, core).start()

    for t in range(16):

        @pl.when(XY_PLACE[t] < place_xy)
        def _():
            tell(near, xy_mate(t))

    @pl.when(y < x)
    def _():
        tell(near, turned)

    for t in range(16):

        @pl.when(Z_LEVEL[t] < rank)
        def _():
            for dev in z_mates(t):
                tell(along, dev)

    wait_some(near, 15 - place_xy + (x < y).astype(jnp.int32))

    @pl.when(relayed)
    def _():
        for h in range(2):
            relay_copy(h, core).start()

    for h in range(2):
        here = jnp.logical_and(diag, core == h)

        @pl.when(jnp.logical_and(level, jnp.logical_not(here)))
        def _():
            mirror_copy(h, core).start()

        @pl.when(here)
        def _():
            mrecv[h] = mbuf[h]

    jj = prow % 16
    valid = (lane // 64) == (jj // 8)
    spread = (
        lax.broadcasted_iota(jnp.int32, (256, 16), 0) // 16
        == lax.broadcasted_iota(jnp.int32, (256, 16), 1)
    ).astype(BF16)
    by_row = nn(spread, tv[...].astype(F32).astype(BF16))
    at = lax.broadcasted_iota(jnp.int32, (256, 32), 0) % 16
    lane32 = lax.broadcasted_iota(jnp.int32, (256, 32), 1)
    ones = jnp.ones((32, 128), BF16)
    for h in range(2):
        picked = jnp.where(lane32 == at + h * 16, by_row, 0.0).astype(BF16)
        target = nn(picked, ones)
        onehot[h * 256 : (h + 1) * 256, :] = jnp.where(
            jnp.logical_and(valid, (lane % 64).astype(F32) == target), 1.0, 0.0
        )
    wdup[...] = jnp.transpose(wdup_t[...])
    wo_t[...] = jnp.transpose(wo[...])
    inp_t[...] = jnp.transpose(inp[...])
    upd_t[...] = jnp.transpose(upd[...])
    perm = (lane == (jj % 8) * 16 + prow // 16).astype(BF16)

    @pl.when(relayed)
    def _():
        for slot in range(2):
            relay_copy(slot, slot).wait_recv()

    wait_some(far, 2 * first.astype(jnp.int32))

    @pl.when(relayed)
    def _():
        for slot in range(2):
            forward_copy(slot).start()

    @pl.when(jnp.logical_and(first, x == y))
    def _():
        for h in range(2):
            mirror_copy(h, core).start()

    for h in range(2):
        here = jnp.logical_and(diag, core == h)

        @pl.when(jnp.logical_not(here))
        def _():
            mirror_copy(h, h).wait_recv()

        rows = pl.ds(h * 256, 256)
        total = jnp.where(valid, logit[rows, :] + nn(perm, mrecv[h]), -1e30)
        shifted = jnp.exp(total - jnp.max(total, axis=-1, keepdims=True))
        probs = shifted / jnp.sum(shifted, axis=-1, keepdims=True)
        grad = (probs - onehot[rows, :]).astype(BF16).astype(F32)
        cotangent = (grad + grad).astype(BF16)
        cot[rows, :] = cotangent
        d_updated = nn(cotangent, wdup_t[...])
        dupd[rows, :] = d_updated
        dupb[rows, :] = d_updated.astype(BF16)

    lead = 1 - core

    def core_copy(k, src, dst):
        return pltpu.make_async_remote_copy(
            src_ref=src.at[k],
            dst_ref=dst.at[k],
            send_sem=cs.at[k],
            recv_sem=cr.at[k],
            device_id=other,
            device_id_type=MESH,
        )

    def out_and_head(send):
        dupb_t[...] = nt(wdup[...], cot[...]).astype(BF16)
        g_head = nn(upd_t[...], cot[...])
        heads[...] = g_head + pltpu.roll(g_head, 64, 1)
        for k in FAR_FIRST:
            to = lax.rem(x + k, 4)
            top = pl.multiple_of(to * 32, 32)
            packed = jnp.where(
                lane[:16] < 64, heads[pl.ds(top, 16), :], heads[pl.ds(top + 16, 16), :]
            ).astype(BF16)
            cols = pl.ds(pl.multiple_of(to * 128, 128), 128)
            g_out = nn(dupb_t[...], hidden[:, cols]).astype(BF16)
            for b in range(4):
                part_b[k, b, 0:32, :] = g_out[32 * b : 32 * b + 32]
                part_b[k, b, 32:48, :] = packed
            if send:
                core_copy(k, part_b, crecv_b).start()

    def gate_and_up(send):
        for h in range(2):
            rows = pl.ds(h * 256, 256)
            for n in range(2):
                cols = slice(n * 256, (n + 1) * 256)
                d_hidden = nn(dupb[rows, :], wo_t[:, cols])
                dgate[rows, cols] = (d_hidden * slope[rows, cols]).astype(BF16)
                dup[rows, cols] = (d_hidden * swish[rows, cols]).astype(BF16)
        for k in FAR_FIRST:
            cols = pl.ds(pl.multiple_of(lax.rem(y + k, 4) * 128, 128), 128)
            g_gate = nn(inp_t[...], dgate[:, cols]).astype(BF16)
            g_up = nn(inp_t[...], dup[:, cols]).astype(BF16)
            for a in range(4):
                part_a[k, a, 0:32, :] = g_gate[32 * a : 32 * a + 32]
                part_a[k, a, 32:64, :] = g_up[32 * a : 32 * a + 32]
            if send:
                core_copy(k, part_a, crecv_a).start()

    def xy_copy(k, src, dst):
        dx, dy = k // 4, k % 4
        if src is xbuf_a:
            piece = src.at[dy, lax.rem(x + dx, 4)]
        else:
            piece = src.at[dx, lax.rem(y + dy, 4)]
        return pltpu.make_async_remote_copy(
            src_ref=piece,
            dst_ref=dst.at[k - 1],
            send_sem=xs.at[k - 1],
            recv_sem=xr.at[k - 1],
            device_id=xy_dev(k),
            device_id_type=MESH,
        )

    def spread_plane(part, crecv, xbuf, xrecv):
        for k in FAR_FIRST:
            core_copy(k, part, crecv).wait_recv()
            for n in range(4):
                xbuf[k, n] = (part[k, n].astype(F32) + crecv[k, n].astype(F32)).astype(BF16)
            for n in FAR_FIRST:
                step = n * 4 + k if xbuf is xbuf_a else k * 4 + n
                if step > 0:
                    xy_copy(step, xbuf, xrecv).start()

    def gather_plane(own, xbuf, xrecv):
        total = own.astype(F32)
        for k in reversed(XY_ORDER):
            xy_copy(k, xbuf, xrecv).wait_recv()
            total = total + xrecv[k - 1].astype(F32)
        return total

    @pl.when(lead == 0)
    def _():
        out_and_head(True)
        gate_and_up(False)
        spread_plane(part_a, crecv_a, xbuf_a, xrecv_a)

    @pl.when(lead == 1)
    def _():
        gate_and_up(True)
        out_and_head(False)
        spread_plane(part_b, crecv_b, xbuf_b, xrecv_b)

    for h in range(2):
        rows = pl.ds(h * 256, 256)
        d_inputs = nt(dgate[rows, :], wg[...]) + nt(dup[rows, :], wu[...])
        nrm = normed[rows, :]
        d_norm = (
            d_inputs
            - jnp.mean(d_inputs, axis=-1, keepdims=True)
            - nrm * jnp.mean(d_inputs * nrm, axis=-1, keepdims=True)
        ) * sinv[rows, :]
        dp_out[:, h * 16 : (h + 1) * 16, :] = (
            (dupd[rows, :] + d_norm).astype(BF16).reshape(16, 16, 128)
        )

    @pl.when(lead == 0)
    def _():
        red[...] = gather_plane(xbuf_a[0, x], xbuf_a, xrecv_a)

    @pl.when(lead == 1)
    def _():
        red[0:48, :] = gather_plane(xbuf_b[0, y], xbuf_b, xrecv_b)

    half = lane[:8] // 64
    for to in range(16):
        own = jnp.where(lead == 0, to // 4, to % 4)
        keep = jnp.where(lead == 0, to % 4 // 2, to // 4 // 2)
        top = pl.multiple_of(8 * own, 8)
        second = pl.multiple_of(32 + 8 * jnp.where(lead == 0, to // 4, to // 4 % 2), 8)
        zbuf[to] = jnp.where(
            half == keep, red[pl.ds(top, 8), :], pltpu.roll(red[pl.ds(second, 8), :], 64, 1)
        ).astype(BF16)

    def z_copy(k, q):
        return pltpu.make_async_remote_copy(
            src_ref=zbuf.at[(z + k) % 16],
            dst_ref=zrecv.at[lead, k],
            send_sem=zs.at[q, k],
            recv_sem=zr.at[lead, k],
            device_id=z_dev(k, q),
            device_id_type=MESH,
        )

    def z_arrival(k, p):
        return pltpu.make_async_remote_copy(
            src_ref=zbuf.at[k],
            dst_ref=zrecv.at[p, k],
            send_sem=zs.at[0, k],
            recv_sem=zr.at[p, k],
            device_id=other,
            device_id_type=MESH,
        )

    wait_some(along, 2 * (15 - mates))
    z_copies = [z_copy(k, q) for k, q in Z_ORDER]
    for copy in z_copies:
        copy.start()
    zrecv[lead, 0] = zbuf[z]
    z_arrival(0, core).wait_recv()
    total = zrecv[:, 0].astype(F32)
    for k in sorted(range(1, 16), key=lambda k: min(k, 16 - k)):
        z_arrival(k, 0).wait_recv()
        z_arrival(k, 1).wait_recv()
        total = total + zrecv[:, k].astype(F32)
    fin_out[...] = total * (1.0 / 512.0)

    @pl.when(relayed)
    def _():
        for slot in range(2):
            relay_copy(slot, core).wait_send()
            forward_copy(slot).wait_send()

    for h in range(2):
        here = jnp.logical_and(diag, core == h)

        @pl.when(jnp.logical_not(jnp.logical_or(here, relayed)))
        def _():
            mirror_copy(h, core).wait_send()

    @pl.when(lead == 0)
    def _():
        for k in range(4):
            core_copy(k, part_b, crecv_b).wait_send()
        for k in XY_ORDER:
            xy_copy(k, xbuf_a, xrecv_a).wait_send()

    @pl.when(lead == 1)
    def _():
        for k in range(4):
            core_copy(k, part_a, crecv_a).wait_send()
        for k in XY_ORDER:
            xy_copy(k, xbuf_b, xrecv_b).wait_send()

    for copy in z_copies:
        copy.wait_send()


def finish(
    dp_in, fin, dp_out, gg_out, gu_out, go_out, gh_out, gg, gu, go, gh, sem
):
    stores = [
        pltpu.make_async_copy(src, dst, sem.at[n])
        for n, (src, dst) in enumerate(
            ((dp_in, dp_out), (gg, gg_out), (gu, gu_out), (go, go_out), (gh, gh_out))
        )
    ]
    stores[0].start()
    r = lax.axis_index("row")
    c = lax.axis_index("col")
    chip, core = lax.div(r, 2), lax.rem(r, 2)
    zh, y, zl = lax.rem(chip, 4), lax.div(c, 4), lax.rem(c, 4)
    a_tile = pltpu.roll(fin[0], lax.rem(128 - 32 * zl, 128), 1)
    gg[...] = jnp.where(core == 0, a_tile[0:4, 0:32], a_tile[4:8, 0:32])
    gu[...] = jnp.where(core == 0, a_tile[0:4, 64:96], a_tile[4:8, 64:96])
    b_tile = fin[1]
    go[...] = pltpu.roll(b_tile, lax.rem(128 - (32 * zh + 16 * core), 128), 1)[:, :16]
    at = 64 * lax.div(zh, 2) + 16 * y + 4 * zl
    h_tile = pltpu.roll(b_tile, lax.rem(192 - at, 128), 1)
    gh[...] = jnp.where(core == 0, h_tile[0:4, :4], h_tile[4:8, :4])
    for store in stores[1:]:
        store.start()
    for store in stores:
        store.wait()


def body(pair, targets, w_gate, w_up, w_out, w_head):
    vm = pltpu.VMEM
    dma = pltpu.SemaphoreType.DMA
    anywhere = pl.BlockSpec(memory_space=pl.ANY)
    vmem = pl.BlockSpec(memory_space=pltpu.VMEM)
    d_pair, fin = pl.pallas_call(
        kernel,
        out_shape=(
            pltpu.VMEM((16, 32, 128), BF16),
            pltpu.VMEM((2, 8, 128), F32),
        ),
        in_specs=[anywhere] * 6,
        out_specs=(vmem, vmem),
        scratch_shapes=[
            vm((16, 32, 128), BF16),
            vm((16, 32), jnp.int32),
            vm((128, 512), BF16),
            vm((128, 512), BF16),
            vm((512, 128), BF16),
            vm((128, 128), BF16),
            vm((128, 128), BF16),
            vm((128, 512), BF16),
            vm((512, 128), BF16),
            vm((128, 512), BF16),
            vm((512, 128), F32),
            vm((512, 128), F32),
            vm((512, 512), BF16),
            vm((512, 512), F32),
            vm((512, 512), F32),
            vm((512, 128), BF16),
            vm((128, 512), BF16),
            vm((512, 128), F32),
            vm((2, 128, 128), BF16),
            vm((2, 128, 128), BF16),
            vm((512, 128), F32),
            vm((512, 128), BF16),
            vm((512, 128), F32),
            vm((512, 128), BF16),
            vm((128, 512), BF16),
            vm((512, 512), BF16),
            vm((512, 512), BF16),
            vm((4, 4, 64, 128), BF16),
            vm((4, 4, 48, 128), BF16),
            vm((4, 4, 64, 128), BF16),
            vm((4, 4, 48, 128), BF16),
            vm((4, 4, 64, 128), BF16),
            vm((4, 4, 48, 128), BF16),
            vm((15, 64, 128), BF16),
            vm((15, 48, 128), BF16),
            vm((128, 128), F32),
            vm((64, 128), F32),
            vm((16, 8, 128), BF16),
            vm((2, 16, 8, 128), BF16),
            dma((6,)),
            dma((2,)),
            dma((2,)),
            dma((4,)),
            dma((4,)),
            dma((15,)),
            dma((15,)),
            dma((2, 16)),
            dma((2, 16)),
            vm((2, 128, 128), BF16),
            dma((2,)),
            dma((2,)),
            dma((2,)),
            pltpu.SemaphoreType.REGULAR,
            pltpu.SemaphoreType.REGULAR,
            pltpu.SemaphoreType.REGULAR,
        ],
        compiler_params=pltpu.CompilerParams(
            collective_id=0, has_side_effects=True
        ),
    )(pair, targets, w_gate, w_up, w_out, w_head.T)
    d_pair, g_gate, g_up, g_out, g_head = pl.pallas_call(
        finish,
        out_shape=(
            jax.ShapeDtypeStruct((16, 32, 128), BF16),
            jax.ShapeDtypeStruct((4, 32), F32),
            jax.ShapeDtypeStruct((4, 32), F32),
            jax.ShapeDtypeStruct((8, 16), F32),
            jax.ShapeDtypeStruct((4, 4), F32),
        ),
        in_specs=[vmem, vmem],
        out_specs=(anywhere,) * 5,
        scratch_shapes=[vm((4, 32), F32), vm((4, 32), F32), vm((8, 16), F32), vm((4, 4), F32), dma((5,))],
        compiler_params=pltpu.CompilerParams(vmem_limit_bytes=16 * 2**20),
    )(d_pair, fin)
    return d_pair, g_gate, g_up, g_out.T, g_head


def solution(mesh):
    placed = (P("row", "col", None), P("row", "col"), P(), P(), P(), P())
    return jax.shard_map(
        body,
        mesh=mesh,
        in_specs=placed,
        out_specs=(
            P("row", "col", None),
            P("row", "col"),
            P("row", "col"),
            P("row", "col"),
            P("row", "col"),
        ),
        check_vma=False,
    )
```
